512 devices in a mesh: fsdp: 16 (over z), expert: 32 (over y, x, core).
Axes of the slice: x: 4, y: 4, z: 16, core: 2. Of those that a mesh axis runs over, the one named last changes fastest.
Arguments:
- tokens: bfloat16 [65536, 1024], P(('fsdp', 'expert')), may hold values from -6 to 6
- attention_gain: float32 [1024], replicated, may hold values from 0.1 to 1.9
- attention_in: bfloat16 [1024, 3072], P(('fsdp', 'expert')), may hold values from -0.1875 to 0.1875
- attention_out: bfloat16 [1024, 1024], P(('fsdp', 'expert')), may hold values from -0.1875 to 0.1875
- expert_gain: float32 [1024], replicated, may hold values from 0.1 to 1.9
- routes: int32 [65536, 6], P(('fsdp', 'expert')), may hold values from 0 to 31, all different within a row; in each aligned block of 128 rows (0 to 127, 128 to 255, ...) at most 30 rows name the same one
- route_weights: float32 [65536, 6], P(('fsdp', 'expert')), may hold values from 0.1 to 1
- gate_weight: bfloat16 [32, 1024, 704], P('expert'), may hold values from -0.1875 to 0.1875
- up_weight: bfloat16 [32, 1024, 704], P('expert'), may hold values from -0.1875 to 0.1875
- down_weight: bfloat16 [32, 704, 1024], P('expert'), may hold values from -0.21875 to 0.21875
Outputs:
- mixed: bfloat16 [65536, 1024], P(('fsdp', 'expert'))
The draws below stay inside these ranges and needn't reach their ends.
Inputs may be any that keep to these rules, and one draw needn't show every extreme that they name: `routes`: the 6 experts of a token differ. Among the token-expert pairs of the tokens of one device, no expert is named more than 30 times, a bound that some block reaches.
All inputs are finite; a program needn't handle non-finite values.
Results may differ from the reference program's by a relative error of at most 0.0075.
Values may be sent and summed in bfloat16 or wider, within the bound.
A program may use at most 64 MiB of HBM per device.

```python
import math
import jax
import jax.numpy as jnp
import numpy as np
from jax import lax

D = 1024
HEADS = 8
HEAD_DIM = 128
FF = 704
TOP = 6
TOK_DEV = 128
EXPERTS = 32
CAP = 30
TOKENS = 65536


def steps_of(own_key, shape, cuts, smallest, top_value):
    def one(dim, blocks):
        heights = jax.random.uniform(jax.random.fold_in(jax.random.fold_in(own_key, 6), dim), (blocks,), jnp.float32, smallest / len(cuts), top_value / len(cuts))
        return jnp.repeat(jnp.exp(heights), shape[dim] // blocks).reshape((-1,) + (1,) * (len(shape) - dim - 1))

    loudness = one(*cuts[0])
    for cut in cuts[1:]:
        loudness = loudness * one(*cut)
    return loudness


def shared_out(stream_key, own, number, rows, number_of, top, bound, skew):
    order = jax.random.permutation(stream_key, number_of)
    crowded, usual = shares(number_of, rows * top, bound, skew, True), shares(number_of, rows * top, bound, skew, False)
    places = jnp.arange(number_of)

    def named(sizes, turn):
        used = int((sizes > 0).sum())
        fixed = max(1, used // 4)
        passed = fixed + (places - fixed + turn * (used - fixed)) % max(1, number_of - fixed)
        return jnp.zeros((number_of,), jnp.int32).at[order[jnp.where(places < fixed, places, passed)]].set(jnp.asarray(sizes, jnp.int32))

    sizes = jnp.where(number % 4 == 0, named(crowded, number // 4), named(usual, number - number // 4 - 1))
    mixed = jax.random.permutation(jax.random.fold_in(own, 3), number_of)
    giver, receiver = mixed[0:number_of // 2 * 2:2], mixed[1:number_of // 2 * 2:2]
    room = jnp.minimum(sizes[giver] - 1, bound - sizes[receiver]) // 2
    room = jnp.where((giver == order[0]) | (receiver == order[0]) | (sizes[receiver] == 0), 0, jnp.maximum(room, 0))
    passed = jax.random.randint(jax.random.fold_in(own, 4), (number_of // 2,), 0, 1 << 20) % (room + 1)
    sizes = sizes.at[giver].add(-passed).at[receiver].add(passed)
    labels = jnp.searchsorted(jnp.cumsum(sizes), jnp.arange(rows * top), side="right").astype(jnp.int32)
    table = labels.reshape(top, rows).T
    table = table[jax.random.permutation(jax.random.fold_in(own, 1), rows)]
    turn = jax.random.randint(jax.random.fold_in(own, 2), (rows, 1), 0, top)
    return jnp.take_along_axis(table, (jnp.arange(top)[None, :] + turn) % top, axis=1)


def shares(count, total, limit, slope, full):
    portions = [(1 << 20) // math.isqrt(rank ** slope) + 1 for rank in range(1, count + 1)]
    largest = limit if full else min(limit, max(-(-total // count), total * portions[0] // sum(portions)))
    least = 1 if total - largest >= count - 1 else 0
    given, surplus = [largest] + [least] * (count - 1), total - largest - least * (count - 1)
    while surplus > 0:
        movable = [i for i in range(1, count) if given[i] < largest] or [i for i in range(1, count) if given[i] < limit]
        pool, budget = sum([portions[i] for i in movable]), surplus
        for i in movable:
            addition = min(limit - given[i], max(1, budget * portions[i] // pool), surplus)
            given[i] = given[i] + addition
            surplus = surplus - addition
    return np.array(given)


def normal_values(stream_key, extent, deviation, limit, pieces=(), kind=jnp.bfloat16):
    level = steps_of(stream_key, extent, pieces, -0.22, 0.18) if pieces else 1.0
    result = jax.random.normal(stream_key, extent, jnp.float32) * deviation * level
    return jnp.minimum(jnp.maximum(result, -limit), limit).astype(kind)


def setup_inputs(seed: int = 0) -> dict:
    streams_of = jax.random.split(jax.random.key(seed), 11)
    tokens = normal_values(streams_of[0], (TOKENS, D), 1.0, 6.0, ((0, 512),))
    attention_gain = jnp.clip(1.0 + 0.18 * jax.random.normal(streams_of[1], (D,), jnp.float32), 0.1, 1.9)
    attention_in = normal_values(streams_of[2], (D, 3 * HEADS * HEAD_DIM), D ** -0.5, 0.1875, ((0, 512),))
    attention_out = normal_values(streams_of[3], (D, HEADS * HEAD_DIM), (HEADS * HEAD_DIM) ** -0.5, 0.1875, ((0, 512),))
    expert_gain = jnp.clip(1.0 + 0.18 * jax.random.normal(streams_of[4], (D,), jnp.float32), 0.1, 1.9)
    routes_keys = jax.random.split(jax.random.fold_in(streams_of[5], 1), TOKENS // TOK_DEV)
    routes_turns = jax.random.permutation(jax.random.fold_in(streams_of[5], 3), TOKENS // TOK_DEV)
    routes = jax.vmap(lambda own, number: shared_out(jax.random.fold_in(streams_of[5], 2), own, number, TOK_DEV, EXPERTS, TOP, CAP, 2))(routes_keys, routes_turns).reshape((TOKENS, TOP))
    route_weights = jnp.clip(0.1 + 0.9 * jax.random.uniform(streams_of[6], (TOKENS, TOP), jnp.float32) ** steps_of(streams_of[6], (TOKENS, TOP), ((0, 512),), -0.2, 0.2), 0.1, 1.0)
    gate_weight = normal_values(streams_of[7], (EXPERTS, D, FF), D ** -0.5, 0.1875, ((0, 32),))
    up_weight = normal_values(streams_of[8], (EXPERTS, D, FF), D ** -0.5, 0.1875, ((0, 32),))
    down_weight = normal_values(streams_of[9], (EXPERTS, FF, D), FF ** -0.5, 0.21875, ((0, 32),))
    return {"tokens": tokens, "attention_gain": attention_gain, "attention_in": attention_in, "attention_out": attention_out, "expert_gain": expert_gain, "routes": routes, "route_weights": route_weights, "gate_weight": gate_weight, "up_weight": up_weight, "down_weight": down_weight}


def rms_scale(inputs, scale_gain):
    mean_square = lax.optimization_barrier(jnp.mean(inputs * inputs, axis=-1, keepdims=True))
    return inputs * lax.rsqrt(mean_square + 1e-06) * scale_gain

def reference(tokens, attention_gain, attention_in, attention_out, expert_gain, routes, route_weights, gate_weight, up_weight, down_weight):
    stream = tokens.astype(jnp.float32)
    normed = rms_scale(stream, attention_gain).astype(jnp.bfloat16)
    projected = jnp.dot(normed, attention_in, preferred_element_type=jnp.float32).astype(jnp.bfloat16)
    sequences = TOKENS // TOK_DEV
    split_heads = projected.reshape(sequences, TOK_DEV, 3, HEADS, HEAD_DIM).astype(jnp.float32)
    queries = split_heads[:, :, 0]
    key_rows = split_heads[:, :, 1]
    value_rows = split_heads[:, :, 2]
    scores = jnp.einsum('sqhd,skhd->shqk', queries, key_rows) / math.sqrt(HEAD_DIM)
    causal = jnp.arange(TOK_DEV)[:, None] >= jnp.arange(TOK_DEV)[None, :]
    raised = jnp.where(causal, jnp.exp(jnp.where(causal, scores, 0.0)), 0.0)
    attention_probs = (raised / lax.optimization_barrier(jnp.sum(raised, axis=-1, keepdims=True))).astype(jnp.bfloat16)
    heads_out = jnp.einsum('shqk,skhd->sqhd', attention_probs.astype(jnp.float32), value_rows).astype(jnp.bfloat16)
    heads_out = heads_out.reshape(TOKENS, HEADS * HEAD_DIM)
    attended = lax.dot_general(heads_out, attention_out, (((1,), (1,)), ((), ())), preferred_element_type=jnp.float32)
    hidden_stream = stream + attended
    expert_in = rms_scale(hidden_stream, expert_gain).astype(jnp.bfloat16)
    pair_count = TOKENS * TOP
    flat_routes = routes.reshape(pair_count).astype(jnp.int32)
    flat_weights = route_weights.reshape(pair_count)
    sorted_pairs = jnp.argsort(flat_routes, stable=True).astype(jnp.int32)
    expert_ids = jnp.arange(EXPERTS, dtype=jnp.int32)
    counts = lax.optimization_barrier(jnp.sum((flat_routes[:, None] == expert_ids[None, :]).astype(jnp.int32), axis=0, dtype=jnp.int32))
    starts = jnp.cumsum(counts, dtype=jnp.int32) - counts
    slot_limit = TOKENS // TOK_DEV * CAP
    offsets = jnp.arange(slot_limit, dtype=jnp.int32)

    def one_expert(running, packed):
        expert_index, gate_block, up_block, down_block = packed
        position = starts[expert_index] + offsets
        live_slot = offsets < counts[expert_index]
        pair_index = sorted_pairs[jnp.minimum(position, pair_count - 1)]
        token_index = (pair_index // TOP).astype(jnp.int32)
        chosen = expert_in[token_index].astype(jnp.float32)
        gate_value = jnp.dot(chosen, gate_block.astype(jnp.float32), precision=lax.Precision.HIGHEST)
        up_value = jnp.dot(chosen, up_block.astype(jnp.float32), precision=lax.Precision.HIGHEST)
        inner_hidden = (jax.nn.silu(gate_value) * up_value).astype(jnp.bfloat16)
        output = jnp.dot(inner_hidden.astype(jnp.float32), down_block.astype(jnp.float32), precision=lax.Precision.HIGHEST).astype(jnp.bfloat16)
        pair_scale = jnp.where(live_slot, flat_weights[pair_index], 0.0)
        running = running.at[token_index].add(pair_scale[:, None] * output.astype(jnp.float32))
        return (running, None)
    moe_total, _ = lax.scan(one_expert, jnp.zeros((TOKENS, D), jnp.float32), (expert_ids, gate_weight, up_weight, down_weight))
    return (hidden_stream + moe_total).astype(jnp.bfloat16)
```

```python
import functools
import math

import jax
import jax.numpy as jnp
from jax import lax
from jax.experimental import pallas as pl
from jax.experimental.pallas import tpu as pltpu
from jax.sharding import PartitionSpec as P

MESH = pl.DeviceIdType.MESH
HEAD_DIM = 128
NX, NY, NZ = 4, 4, 16


def rms_scale(inputs, scale_gain):
    mean_square = jnp.mean(inputs * inputs, axis=-1, keepdims=True)
    return inputs * lax.rsqrt(mean_square + 1e-06) * scale_gain


def place():
    z = lax.axis_index("fsdp")
    e = lax.axis_index("expert")
    core = e % 2
    x = (e // 2) % NX
    y = e // (2 * NX)
    return x, y, z, core


def expert_at(x, y, core):
    return (y * NX + x) * 2 + core


def gather_kernel(
    a_ref,
    n_ref,
    g_ref,
    x2_ref,
    ex,
    ex_send,
    ex_recv,
    n_sem,
    z_send,
    z_recv,
    p2_send,
    p2_recv,
    p3_send,
    p3_recv,
):
    x, y, z, core = place()
    j = 2 * x + core
    half = NZ // 2

    def at(dx=0, dy=0, dz=0):
        ident = {}
        if dz:
            ident["fsdp"] = (z + dz + NZ) % NZ
        if dx or dy:
            ident["expert"] = expert_at((x + dx + NX) % NX, (y + dy + NY) % NY, core)
        return ident

    def peer(d):
        return {"expert": y * 2 * NX + (j + d) % 8}

    barrier = pltpu.get_barrier_semaphore()
    partners = [peer(d) for d in range(1, 8)] + [at(dy=1), at(dy=-1), at(dz=1), at(dz=-1)]
    for ident in partners:
        pl.semaphore_signal(barrier, inc=1, device_id=ident, device_id_type=MESH)
    pl.semaphore_wait(barrier, len(partners))

    def remote(src, dst, send, recv, ident):
        return pltpu.make_async_remote_copy(
            src_ref=src, dst_ref=dst, send_sem=send, recv_sem=recv, device_id=ident, device_id_type=MESH
        )

    sent = []

    def go(copy):
        copy.start()
        sent.append(copy)
        return copy

    swaps = []
    for d in range(1, 8):
        swaps.append(
            go(remote(a_ref.at[(j + d) % 8], ex.at[j], ex_send.at[d - 1], ex_recv.at[d - 1], peer(d)))
        )
    sibling = {"expert": y * 2 * NX + 2 * x + 1 - core}
    rows_copy = go(remote(n_ref, x2_ref.at[core], n_sem.at[0], n_sem.at[1], sibling))
    own_rows = pltpu.make_async_copy(n_ref, x2_ref.at[core], n_sem.at[2])
    own_rows.start()
    own = pltpu.make_async_copy(a_ref.at[j], ex.at[j], n_sem.at[3])
    own.start()
    own.wait()
    for copy in swaps:
        copy.wait_recv()
    pieces = [ex[i].astype(jnp.float32) for i in range(8)]
    g_ref[x, z, y] = jnp.concatenate(pieces, axis=0).astype(jnp.bfloat16)

    def chunks(s):
        found = []
        if 0 <= s <= half - 1:
            found.append((0, s, (z - s + NZ) % NZ))
        if 1 <= s <= half:
            found.append((1, s, (z + s) % NZ))
        return found

    def slot(color, s):
        return s if color == 0 else half + s - 1

    def slab(color, along, across, zs):
        return g_ref.at[across, zs, along] if color == 0 else g_ref.at[along, zs, across]

    live = {}
    for it in range(half + 5):
        s = it
        if s == 0:
            mine = g_ref.at[x, z, y]
            live["z", 0, 1] = go(remote(mine, mine, z_send.at[slot(0, 1)], z_recv.at[slot(0, 1)], at(dz=1)))
            live["z", 1, 1] = go(remote(mine, mine, z_send.at[slot(1, 1)], z_recv.at[slot(1, 1)], at(dz=-1)))
        for color, _, zs in chunks(s):
            if s >= 1:
                live["z", color, s].wait_recv()
            here = g_ref.at[x, zs, y]
            last = half - 1 if color == 0 else half
            if 1 <= s < last:
                k = slot(color, s + 1)
                live["z", color, s + 1] = go(
                    remote(here, here, z_send.at[k], z_recv.at[k], at(dz=1 if color == 0 else -1))
                )
            k = slot(color, s)
            for i, d in enumerate((1, -1)):
                ident = at(dy=d) if color == 0 else at(dx=d)
                live["p2", color, s, i] = go(remote(here, here, p2_send.at[k, i], p2_recv.at[k, i], ident))
        s = it - 1
        for color, _, zs in chunks(s):
            k = slot(color, s)
            live["p2", color, s, 0].wait_recv()
            live["p2", color, s, 1].wait_recv()
            d = 1 if s % 2 == 0 else -1
            along, across = (y, x) if color == 0 else (x, y)
            block = slab(color, (along - d + 4) % 4, across, zs)
            ident = at(dy=d) if color == 0 else at(dx=d)
            live["p2", color, s, 2] = go(remote(block, block, p2_send.at[k, 2], p2_recv.at[k, 2], ident))
        s = it - 2
        for color, _, zs in chunks(s):
            k = slot(color, s)
            live["p2", color, s, 2].wait_recv()
            block = g_ref.at[x, zs] if color == 0 else g_ref.at[:, zs, y]
            for i, d in enumerate((1, -1)):
                ident = at(dx=d) if color == 0 else at(dy=d)
                live["p3", color, s, i] = go(remote(block, block, p3_send.at[k, i], p3_recv.at[k, i], ident))
        s = it - 3
        for color, _, zs in chunks(s):
            k = slot(color, s)
            live["p3", color, s, 0].wait_recv()
            live["p3", color, s, 1].wait_recv()
            for i, d in enumerate((1, -1)):
                part = pl.ds(2 * i, 2)
                if color == 0:
                    block = g_ref.at[(x - d + 4) % 4, zs, part]
                    ident = at(dx=d)
                else:
                    block = g_ref.at[part, zs, (y - d + 4) % 4]
                    ident = at(dy=d)
                live["p3", color, s, 2 + i] = go(
                    remote(block, block, p3_send.at[k, 2 + i], p3_recv.at[k, 2 + i], ident)
                )
        s = it - 4
        for color, _, zs in chunks(s):
            live["p3", color, s, 2].wait_recv()
            live["p3", color, s, 3].wait_recv()
    rows_copy.wait_recv()
    own_rows.wait()
    for copy in sent:
        copy.wait_send()


def attention_kernel(g_ref, x2_ref, out_ref):
    rows = x2_ref[...].reshape(256, 1024)
    causal = lax.broadcasted_iota(jnp.int32, (128, 128), 0) >= lax.broadcasted_iota(jnp.int32, (128, 128), 1)
    heads = [[], []]
    for h in range(NX):
        weight = g_ref[h, :, :, :, 0:384].reshape(1024, 384)
        qkv = jnp.dot(rows, weight, preferred_element_type=jnp.float32).astype(jnp.bfloat16)
        for s in range(2):
            part = qkv[s * 128 : (s + 1) * 128]
            q, k, v = part[:, 0:128], part[:, 128:256], part[:, 256:384]
            scores = lax.dot_general(
                q, k, (((1,), (1,)), ((), ())), preferred_element_type=jnp.float32
            ) / math.sqrt(HEAD_DIM)
            raised = jnp.where(causal, jnp.exp(jnp.where(causal, scores, 0.0)), 0.0)
            probs = (raised / jnp.sum(raised, axis=-1, keepdims=True)).astype(jnp.bfloat16)
            heads[s].append(jnp.dot(probs, v, preferred_element_type=jnp.float32).astype(jnp.bfloat16))
    total = jnp.zeros((256, 1024), jnp.float32)
    for h in range(NX):
        both = jnp.concatenate([heads[0][h], heads[1][h]], axis=0)
        weight = g_ref[h, :, :, :, 384:512].reshape(1024, 128)
        total = total + lax.dot_general(
            both, weight, (((1,), (1,)), ((), ())), preferred_element_type=jnp.float32
        )
    out_ref[0] = total[0:128]
    out_ref[1] = total[128:256]


def swap_kernel(part_ref, tok_ref, out_ref, buf, sems):
    x, y, z, core = place()
    sibling = {"expert": expert_at(x, y, 1 - core)}
    barrier = pltpu.get_barrier_semaphore()
    pl.semaphore_signal(barrier, inc=1, device_id=sibling, device_id_type=MESH)
    pl.semaphore_wait(barrier, 1)
    copy = pltpu.make_async_remote_copy(
        src_ref=part_ref.at[1 - core],
        dst_ref=buf,
        send_sem=sems.at[0],
        recv_sem=sems.at[1],
        device_id=sibling,
        device_id_type=MESH,
    )
    copy.start()
    stream = tok_ref[...].astype(jnp.float32) + part_ref[core]
    copy.wait()
    out_ref[...] = stream + buf[...]


VMEM = pl.BlockSpec(memory_space=pltpu.VMEM)
DMA = pltpu.SemaphoreType.DMA


def per_device(
    tokens,
    attention_gain,
    attention_in,
    attention_out,
    expert_gain,
    routes,
    route_weights,
    gate_weight,
    up_weight,
    down_weight,
):
    row_count = tokens.shape[0]
    model_width = tokens.shape[1]
    stream = tokens.astype(jnp.float32)
    normed = rms_scale(stream, attention_gain).astype(jnp.bfloat16)
    pieces = jnp.concatenate(
        [attention_in.reshape(2, 3, 8, 128), attention_out.reshape(2, 1, 8, 128)], axis=1
    )
    pieces = pieces.transpose(2, 0, 1, 3).reshape(8, 2, 512)
    chunk_count = NZ
    weights, both = pl.pallas_call(
        gather_kernel,
        out_shape=(
            jax.ShapeDtypeStruct((NX, NZ, NY, 16, 512), jnp.bfloat16),
            jax.ShapeDtypeStruct((2, row_count, model_width), jnp.bfloat16),
        ),
        in_specs=[VMEM, VMEM],
        out_specs=(VMEM, VMEM),
        scratch_shapes=[
            pltpu.VMEM((8, 2, 512), jnp.bfloat16),
            DMA((7,)),
            DMA((7,)),
            DMA((4,)),
            DMA((chunk_count,)),
            DMA((chunk_count,)),
            DMA((chunk_count, 3)),
            DMA((chunk_count, 3)),
            DMA((chunk_count, 4)),
            DMA((chunk_count, 4)),
        ],
        compiler_params=pltpu.CompilerParams(collective_id=0, has_side_effects=True),
        name="weight_gather",
    )(pieces, normed)
    partial = pl.pallas_call(
        attention_kernel,
        out_shape=jax.ShapeDtypeStruct((2, row_count, model_width), jnp.float32),
        in_specs=[VMEM, VMEM],
        out_specs=VMEM,
        name="attention",
    )(weights, both)
    hidden_stream = pl.pallas_call(
        swap_kernel,
        out_shape=jax.ShapeDtypeStruct((row_count, model_width), jnp.float32),
        in_specs=[VMEM, VMEM],
        out_specs=VMEM,
        scratch_shapes=[pltpu.VMEM((row_count, model_width), jnp.float32), DMA((2,))],
        compiler_params=pltpu.CompilerParams(collective_id=1, has_side_effects=True),
        name="core_swap",
    )(partial, tokens)
    expert_in = rms_scale(hidden_stream, expert_gain).astype(jnp.bfloat16)
    experts_here = lax.axis_size("expert")
    top_count = routes.shape[1]
    capacity = 30
    expert_ids = jnp.arange(experts_here, dtype=jnp.int32)
    named = routes[:, :, None] == expert_ids[None, None, :]
    chosen = jnp.any(named, axis=1)
    weight_of = jnp.sum(jnp.where(named, route_weights[:, :, None], 0.0), axis=1)
    counted = chosen.astype(jnp.bfloat16)
    earlier = (jnp.arange(row_count)[:, None] > jnp.arange(row_count)[None, :]).astype(jnp.bfloat16)
    position = jnp.dot(earlier, counted, preferred_element_type=jnp.float32)
    position = jnp.where(chosen, position, -1.0)
    slots = jnp.arange(capacity, dtype=jnp.float32)
    spread = position[:, :, None] == slots[None, None, :]
    select = spread.reshape(row_count, experts_here * capacity)
    outgoing = lax.dot_general(
        select.astype(jnp.bfloat16), expert_in, (((0,), (0,)), ((), ())), preferred_element_type=jnp.float32
    ).astype(jnp.bfloat16)
    outgoing = outgoing.reshape(experts_here, capacity, model_width)
    arrived = lax.all_to_all(outgoing, "expert", split_axis=0, concat_axis=0, tiled=True)
    flat_in = arrived.reshape(experts_here * capacity, model_width)
    gate_value = jnp.dot(flat_in, gate_weight[0], preferred_element_type=jnp.float32)
    up_value = jnp.dot(flat_in, up_weight[0], preferred_element_type=jnp.float32)
    inner_hidden = (jax.nn.silu(gate_value) * up_value).astype(jnp.bfloat16)
    result = jnp.dot(inner_hidden, down_weight[0], preferred_element_type=jnp.float32).astype(jnp.bfloat16)
    result = result.reshape(experts_here, capacity, model_width)
    returned = lax.all_to_all(result, "expert", split_axis=0, concat_axis=0, tiled=True)
    returned = returned.reshape(experts_here * capacity, model_width)
    scale = jnp.where(spread, weight_of[:, :, None], 0.0).reshape(row_count, experts_here * capacity)
    rounded = lax.reduce_precision(scale, 8, 7)
    high = rounded.astype(jnp.bfloat16)
    low = (scale - rounded).astype(jnp.bfloat16)
    mixture = jnp.dot(high, returned, preferred_element_type=jnp.float32) + jnp.dot(
        low, returned, preferred_element_type=jnp.float32
    )
    return (hidden_stream + mixture).astype(jnp.bfloat16)


def solution(mesh):
    placed = (
        P(("fsdp", "expert"), None),
        P(),
        P(("fsdp", "expert"), None),
        P(("fsdp", "expert"), None),
        P(),
        P(("fsdp", "expert"), None),
        P(("fsdp", "expert"), None),
        P("expert", None, None),
        P("expert", None, None),
        P("expert", None, None),
    )
    return jax.shard_map(
        per_device,
        mesh=mesh,
        in_specs=placed,
        out_specs=P(("fsdp", "expert"), None),
        check_vma=False,
    )
```

```python
import functools
import math

import jax
import jax.numpy as jnp
from jax import lax
from jax.experimental import pallas as pl
from jax.experimental.pallas import tpu as pltpu
from jax.sharding import PartitionSpec as P

MESH = pl.DeviceIdType.MESH
HEAD_DIM = 128
NX, NY, NZ = 4, 4, 16


def rms_scale(inputs, scale_gain):
    mean_square = jnp.mean(inputs * inputs, axis=-1, keepdims=True)
    return inputs * lax.rsqrt(mean_square + 1e-06) * scale_gain


def place():
    z = lax.axis_index("fsdp")
    e = lax.axis_index("expert")
    core = e % 2
    x = (e // 2) % NX
    y = e // (2 * NX)
    return x, y, z, core


def expert_at(x, y, core):
    return (y * NX + x) * 2 + core


def gather_kernel(
    a_ref,
    n_ref,
    g_ref,
    x2_ref,
    ex,
    ex_send,
    ex_recv,
    n_sem,
    z_send,
    z_recv,
    p2_send,
    p2_recv,
    p3_send,
    p3_recv,
):
    x, y, z, core = place()
    j = 2 * x + core
    half = NZ // 2

    def at(dx=0, dy=0, dz=0):
        ident = {}
        if dz:
            ident["fsdp"] = (z + dz + NZ) % NZ
        if dx or dy:
            ident["expert"] = expert_at((x + dx + NX) % NX, (y + dy + NY) % NY, core)
        return ident

    def peer(d):
        return {"expert": y * 2 * NX + (j + d) % 8}

    barrier = pltpu.get_barrier_semaphore()
    partners = [peer(d) for d in range(1, 8)] + [at(dy=1), at(dy=-1), at(dz=1), at(dz=-1)]
    for ident in partners:
        pl.semaphore_signal(barrier, inc=1, device_id=ident, device_id_type=MESH)
    pl.semaphore_wait(barrier, len(partners))

    def remote(src, dst, send, recv, ident):
        return pltpu.make_async_remote_copy(
            src_ref=src, dst_ref=dst, send_sem=send, recv_sem=recv, device_id=ident, device_id_type=MESH
        )

    sent = []

    def go(copy):
        copy.start()
        sent.append(copy)
        return copy

    swaps = []
    for d in range(1, 8):
        swaps.append(
            go(remote(a_ref.at[(j + d) % 8], ex.at[j], ex_send.at[d - 1], ex_recv.at[d - 1], peer(d)))
        )
    sibling = {"expert": y * 2 * NX + 2 * x + 1 - core}
    rows_copy = go(remote(n_ref, x2_ref.at[core], n_sem.at[0], n_sem.at[1], sibling))
    own_rows = pltpu.make_async_copy(n_ref, x2_ref.at[core], n_sem.at[2])
    own_rows.start()
    own = pltpu.make_async_copy(a_ref.at[j], ex.at[j], n_sem.at[3])
    own.start()
    own.wait()
    for copy in swaps:
        copy.wait_recv()
    pieces = [ex[i].astype(jnp.float32) for i in range(8)]
    g_ref[x, z, y] = jnp.concatenate(pieces, axis=0).astype(jnp.bfloat16)

    def chunks(s):
        found = []
        if 0 <= s <= half - 1:
            found.append((0, s, (z - s + NZ) % NZ))
        if 1 <= s <= half:
            found.append((1, s, (z + s) % NZ))
        return found

    def slot(color, s):
        return s if color == 0 else half + s - 1

    def slab(color, along, across, zs):
        return g_ref.at[across, zs, along] if color == 0 else g_ref.at[along, zs, across]

    live = {}
    for it in range(half + 5):
        s = it
        if s == 0:
            mine = g_ref.at[x, z, y]
            live["z", 0, 1] = go(remote(mine, mine, z_send.at[slot(0, 1)], z_recv.at[slot(0, 1)], at(dz=1)))
            live["z", 1, 1] = go(remote(mine, mine, z_send.at[slot(1, 1)], z_recv.at[slot(1, 1)], at(dz=-1)))
        for color, _, zs in chunks(s):
            if s >= 1:
                live["z", color, s].wait_recv()
            here = g_ref.at[x, zs, y]
            last = half - 1 if color == 0 else half
            if 1 <= s < last:
                k = slot(color, s + 1)
                live["z", color, s + 1] = go(
                    remote(here, here, z_send.at[k], z_recv.at[k], at(dz=1 if color == 0 else -1))
                )
            k = slot(color, s)
            for i, d in enumerate((1, -1)):
                ident = at(dy=d) if color == 0 else at(dx=d)
                live["p2", color, s, i] = go(remote(here, here, p2_send.at[k, i], p2_recv.at[k, i], ident))
        s = it - 1
        for color, _, zs in chunks(s):
            k = slot(color, s)
            live["p2", color, s, 0].wait_recv()
            live["p2", color, s, 1].wait_recv()
            d = 1 if s % 2 == 0 else -1
            along, across = (y, x) if color == 0 else (x, y)
            block = slab(color, (along - d + 4) % 4, across, zs)
            ident = at(dy=d) if color == 0 else at(dx=d)
            live["p2", color, s, 2] = go(remote(block, block, p2_send.at[k, 2], p2_recv.at[k, 2], ident))
        s = it - 2
        for color, _, zs in chunks(s):
            k = slot(color, s)
            live["p2", color, s, 2].wait_recv()
            block = g_ref.at[x, zs] if color == 0 else g_ref.at[:, zs, y]
            for i, d in enumerate((1, -1)):
                ident = at(dx=d) if color == 0 else at(dy=d)
                live["p3", color, s, i] = go(remote(block, block, p3_send.at[k, i], p3_recv.at[k, i], ident))
        s = it - 3
        for color, _, zs in chunks(s):
            k = slot(color, s)
            live["p3", color, s, 0].wait_recv()
            live["p3", color, s, 1].wait_recv()
            for i, d in enumerate((1, -1)):
                part = pl.ds(2 * i, 2)
                if color == 0:
                    block = g_ref.at[(x - d + 4) % 4, zs, part]
                    ident = at(dx=d)
                else:
                    block = g_ref.at[part, zs, (y - d + 4) % 4]
                    ident = at(dy=d)
                live["p3", color, s, 2 + i] = go(
                    remote(block, block, p3_send.at[k, 2 + i], p3_recv.at[k, 2 + i], ident)
                )
        s = it - 4
        for color, _, zs in chunks(s):
            live["p3", color, s, 2].wait_recv()
            live["p3", color, s, 3].wait_recv()
    rows_copy.wait_recv()
    own_rows.wait()
    for copy in sent:
        copy.wait_send()


def attention_kernel(g_ref, x2_ref, out_ref):
    rows = x2_ref[...].reshape(256, 1024)
    causal = lax.broadcasted_iota(jnp.int32, (128, 128), 0) >= lax.broadcasted_iota(jnp.int32, (128, 128), 1)
    heads = [[], []]
    for h in range(NX):
        weight = g_ref[h, :, :, :, 0:384].reshape(1024, 384)
        qkv = jnp.dot(rows, weight, preferred_element_type=jnp.float32).astype(jnp.bfloat16)
        for s in range(2):
            part = qkv[s * 128 : (s + 1) * 128]
            q, k, v = part[:, 0:128], part[:, 128:256], part[:, 256:384]
            scores = lax.dot_general(
                q, k, (((1,), (1,)), ((), ())), preferred_element_type=jnp.float32
            ) / math.sqrt(HEAD_DIM)
            raised = jnp.where(causal, jnp.exp(jnp.where(causal, scores, 0.0)), 0.0)
            probs = (raised / jnp.sum(raised, axis=-1, keepdims=True)).astype(jnp.bfloat16)
            heads[s].append(jnp.dot(probs, v, preferred_element_type=jnp.float32).astype(jnp.bfloat16))
    total = jnp.zeros((256, 1024), jnp.float32)
    for h in range(NX):
        both = jnp.concatenate([heads[0][h], heads[1][h]], axis=0)
        weight = g_ref[h, :, :, :, 384:512].reshape(1024, 128)
        total = total + lax.dot_general(
            both, weight, (((1,), (1,)), ((), ())), preferred_element_type=jnp.float32
        )
    out_ref[0] = total[0:128]
    out_ref[1] = total[128:256]


SLOTS = 32
HALF = 512
KS = (0, 1, 3, 2)
SENDS, RECVS = 171, 190


def moe_kernel(
    part_ref,
    tok_ref,
    gain_ref,
    info_ref,
    wg_hbm,
    wu_hbm,
    wd_hbm,
    out_ref,
    swap,
    hidden,
    wg,
    wu,
    wd,
    ibuf,
    g,
    disp,
    r,
    t,
    res,
    cbuf,
    t2,
    sbuf,
    f,
    tf,
    own_sum,
    ss,
    rv,
):
    x, y, z, core = place()
    lines = ((y, x), (x, y))

    def dev(color, dp=0, dd=0, to=None):
        p, d = lines[color]
        p, d = (p + dp + 4) % 4, (d + dd + 4) % 4
        to = core if to is None else to
        return {"expert": expert_at(d, p, to) if color == 0 else expert_at(p, d, to)}

    sibling = {"expert": expert_at(x, y, 1 - core)}
    barrier = pltpu.get_barrier_semaphore()
    partners = [sibling]
    for color in range(2):
        partners += [dev(color, dd=s, to=to) for s in (1, -1) for to in (0, 1)]
        partners.append(dev(color, dp=2))
    for ident in partners:
        pl.semaphore_signal(barrier, inc=1, device_id=ident, device_id_type=MESH)
    pl.semaphore_wait(barrier, len(partners))

    sent, bases = [], {}

    def base(name, width=1):
        if name not in bases:
            bases[name] = sum(w for _, w in bases.values()), width
        return bases[name][0]

    def send(src, dst, name, ident, width=1):
        at = base(name, width)
        copy = pltpu.make_async_remote_copy(
            src_ref=src,
            dst_ref=dst,
            send_sem=ss.at[len(sent)],
            recv_sem=rv.at[at + core if width == 2 else at],
            device_id=ident,
            device_id_type=MESH,
        )
        copy.start()
        sent.append(copy.wait_send)

    def local(src, dst, name):
        copy = pltpu.make_async_copy(src, dst, rv.at[base(name)])
        copy.start()

    def arrive(dst, name, which=0):
        pltpu.make_async_copy(dst, dst, rv.at[base(name) + which]).wait()

    send(part_ref.at[1 - core], swap, "swap", sibling)
    for source, place_in, name in ((wg_hbm, wg, "wg"), (wu_hbm, wu, "wu"), (wd_hbm, wd, "wd")):
        local(source, place_in, name)
    for color in range(2):
        p, d = lines[color]
        for k in (1, 3, 2):
            send(info_ref.at[color, (p + k) % 4], ibuf.at[color, p], ("info", color, k), dev(color, dp=k))
        ibuf[color, p] = info_ref[color, p]
    stream = tok_ref[...].astype(jnp.float32) + part_ref[core]
    arrive(swap, "swap")
    stream = stream + swap[...]
    hidden[...] = stream
    expert_in = rms_scale(stream, gain_ref[...]).astype(jnp.bfloat16)
    g[0, y] = expert_in[:, 0:HALF]
    g[1, x] = expert_in[:, HALF : 2 * HALF]

    for color in range(2):
        p, d = lines[color]
        for k in (1, 3):
            send(g.at[color, p], g.at[color, p], ("g", color, k), dev(color, dp=k))

    def first_relay(color):
        p, d = lines[color]
        arrive(g.at[color, (p + 3) % 4], ("g", color, 1))
        arrive(g.at[color, (p + 1) % 4], ("g", color, 3))
        for i, k in enumerate((1, 3)):
            block = g.at[color, (p - k + 4) % 4, pl.ds(64 * i, 64)]
            send(block, block, ("g2", color, k), dev(color, dp=k))

    def first_last(color):
        p, d = lines[color]
        for i, k in enumerate((1, 3)):
            arrive(g.at[color, (p + 2) % 4, pl.ds(64 * i, 64)], ("g2", color, k))

    slot_ids = lax.broadcasted_iota(jnp.int32, (SLOTS, 128), 0).astype(jnp.float32)

    def spread(color, k, weighted):
        p, d = lines[color]
        info = ibuf[color, (p + k) % 4]
        blocks = []
        for i in range(8):
            hit = info[i : i + 1] == slot_ids
            blocks.append(jnp.where(hit, info[8 + i : 9 + i] if weighted else 1.0, 0.0))
        return jnp.concatenate(blocks, axis=0)

    def sign(k):
        return 1 if k in (0, 3) else -1

    def scatter(kind, color, k, dd, to, src, dst, through):
        name = (kind, color, k, dd)
        if dd == 2:
            send(src, through.at[color, k, core], name, dev(color, dd=sign(k), to=to), width=2)
        else:
            send(src, dst, name, dev(color, dd=dd, to=to), width=2)

    def forward(kind, color, k, through, into):
        p, d = lines[color]
        for from_core in range(2):
            arrive(through.at[color, k, from_core], (kind, color, k, 2), from_core)
            at = base((kind, color, k, "on"), 2)
            copy = pltpu.make_async_remote_copy(
                src_ref=through.at[color, k, from_core],
                dst_ref=into((d - sign(k) + 4) % 4, from_core),
                send_sem=ss.at[len(sent)],
                recv_sem=rv.at[at + from_core],
                device_id=dev(color, dd=sign(k)),
                device_id_type=MESH,
            )
            copy.start()
            sent.append(copy.wait_send)

    def dispatch(color, k):
        p, d = lines[color]
        seq = (p + k) % 4
        rows = jnp.dot(
            spread(color, k, False).astype(jnp.bfloat16), g[color, seq], preferred_element_type=jnp.float32
        ).astype(jnp.bfloat16)
        disp[color, k] = rows.reshape(4, 2, SLOTS, HALF)
        target = r.at[color, d, seq, core]
        for dd in (2, 1, -1):
            for to in range(2):
                scatter("d", color, k, dd, to, disp.at[color, k, (d + dd + 4) % 4, to], target, t)
        send(disp.at[color, k, d, 1 - core], target, ("d", color, k, 0), sibling)
        local(disp.at[color, k, d, core], target, ("d", color, k, "here"))

    def dispatch_forward(color, k):
        p, d = lines[color]
        forward("d", color, k, t, lambda d_from, from_core: r.at[color, d_from, (p + k) % 4, from_core])

    def arrivals(kind, color, k, dd, block):
        if dd == 0:
            arrive(block(core), (kind, color, k, "here"))
            arrive(block(1 - core), (kind, color, k, 0))
            return
        for from_core in range(2):
            name = (kind, color, k, "on" if dd == 2 else -dd)
            arrive(block(from_core), name, from_core)

    def group(k):
        column = (x + k) % 4
        across = {0: 0, 1: 1, 3: -1, 2: 2}[k]
        for kk in KS:
            arrivals("d", 0, kk, across, lambda c: r.at[0, column, (y + kk) % 4, c])
        for dd in (0, 1, -1, 2):
            arrivals("d", 1, k, dd, lambda c: r.at[1, (y + dd + 4) % 4, column, c])
        low = r[0, column].reshape(256, HALF)
        high = r[1, :, pl.ds(column, 1)].reshape(256, HALF)

        def product(weight):
            return jnp.dot(low, weight[0:HALF], preferred_element_type=jnp.float32) + jnp.dot(
                high, weight[HALF : 2 * HALF], preferred_element_type=jnp.float32
            )

        gate, up = product(wg), product(wu)
        inner = (gate / (1.0 + jnp.exp(-gate)) * up).astype(jnp.bfloat16)
        result = jnp.dot(inner, wd[...], preferred_element_type=jnp.float32).astype(jnp.bfloat16)
        res[0, k] = result[:, 0:HALF].reshape(4, 2, SLOTS, HALF)
        res[1, k] = result[:, HALF : 2 * HALF].reshape(4, 2, SLOTS, HALF)
        pairs = [(0, kk, across) for kk in KS] + [(1, k, dd) for dd in (2, 1, -1, 0)]
        for color, kk, dd in pairs:
            p, d = lines[color]
            row = (y + kk) % 4 if color == 0 else (y + dd + 4) % 4
            target = cbuf.at[color, d, core, (p + kk) % 4]
            if dd == 0:
                send(res.at[color, k, row, 1 - core], target, ("r", color, kk, 0), sibling)
                local(res.at[color, k, row, core], target, ("r", color, kk, "here"))
            else:
                for to in range(2):
                    scatter("r", color, kk, dd, to, res.at[color, k, row, to], target, t2)

    def return_forward(color, k):
        p, d = lines[color]
        forward("r", color, k, t2, lambda d_from, from_core: cbuf.at[color, d_from, from_core, (p + k) % 4])

    def combine(color, k):
        p, d = lines[color]
        seq = (p + k) % 4
        for dd in (0, 1, -1, 2):
            arrivals("r", color, k, dd, lambda c: cbuf.at[color, (d + dd + 4) % 4, c, seq])
        scale = spread(color, k, True)
        high = scale.astype(jnp.bfloat16)
        low = (scale - high.astype(jnp.float32)).astype(jnp.bfloat16)
        rows = cbuf[color, :, :, pl.ds(seq, 1)].reshape(256, HALF)
        total = 0.0
        for term in (high, low):
            total = total + lax.dot_general(
                term, rows, (((0,), (0,)), ((), ())), preferred_element_type=jnp.float32
            )
        if k == 0:
            own_sum[color] = total
            return
        sbuf[color, k] = total.astype(jnp.bfloat16)
        if k != 2:
            send(sbuf.at[color, k], f.at[color, k], ("f", color, k), dev(color, dp=k))
            return
        for i, step in enumerate((1, 3)):
            send(
                sbuf.at[color, k, pl.ds(64 * i, 64)], tf.at[color, i], ("f2", color, step), dev(color, dp=step)
            )

    def last_forward(color):
        for i, step in enumerate((1, 3)):
            arrive(tf.at[color, i], ("f2", color, step))
            send(tf.at[color, i], f.at[color, 2, pl.ds(64 * i, 64)], ("f3", color, step), dev(color, dp=step))

    both = (0, 1)
    for color in both:
        dispatch(color, 0)
    for color in both:
        first_relay(color)
    for color in both:
        for k in (1, 3, 2):
            arrive(ibuf.at[color, (lines[color][0] - k + 4) % 4], ("info", color, k))
    for k in (1, 3):
        for color in both:
            dispatch(color, k)
    for color in both:
        dispatch_forward(color, 0)
    for color in both:
        first_last(color)
        dispatch(color, 2)
    for k in (1, 3):
        for color in both:
            dispatch_forward(color, k)
    arrive(wg, "wg")
    arrive(wu, "wu")
    arrive(wd, "wd")
    group(0)
    for color in both:
        dispatch_forward(color, 2)
    group(1)
    return_forward(1, 0)
    group(3)
    return_forward(1, 1)
    group(2)
    return_forward(1, 3)
    for k in (2, 1, 3, 0):
        return_forward(0, k)
    return_forward(1, 2)
    for k in (2, 1, 3):
        for color in both:
            combine(color, k)
    for color in both:
        last_forward(color)
    for color in both:
        combine(color, 0)
    for color in both:
        cols = pl.ds(HALF * color, HALF)
        total = hidden[:, cols] + own_sum[color]
        for k in (1, 3):
            arrive(f.at[color, k], ("f", color, k))
            total = total + f[color, k].astype(jnp.float32)
        for i, step in enumerate((1, 3)):
            arrive(f.at[color, 2, pl.ds(64 * i, 64)], ("f3", color, step))
        total = total + f[color, 2].astype(jnp.float32)
        out_ref[:, cols] = total.astype(jnp.bfloat16)
    for wait in sent:
        wait()


VMEM = pl.BlockSpec(memory_space=pltpu.VMEM)
DMA = pltpu.SemaphoreType.DMA


def per_device(
    tokens,
    attention_gain,
    attention_in,
    attention_out,
    expert_gain,
    routes,
    route_weights,
    gate_weight,
    up_weight,
    down_weight,
):
    row_count = tokens.shape[0]
    model_width = tokens.shape[1]
    stream = tokens.astype(jnp.float32)
    normed = rms_scale(stream, attention_gain).astype(jnp.bfloat16)
    pieces = jnp.concatenate(
        [attention_in.reshape(2, 3, 8, 128), attention_out.reshape(2, 1, 8, 128)], axis=1
    )
    pieces = pieces.transpose(2, 0, 1, 3).reshape(8, 2, 512)
    chunk_count = NZ
    weights, both = pl.pallas_call(
        gather_kernel,
        out_shape=(
            jax.ShapeDtypeStruct((NX, NZ, NY, 16, 512), jnp.bfloat16),
            jax.ShapeDtypeStruct((2, row_count, model_width), jnp.bfloat16),
        ),
        in_specs=[VMEM, VMEM],
        out_specs=(VMEM, VMEM),
        scratch_shapes=[
            pltpu.VMEM((8, 2, 512), jnp.bfloat16),
            DMA((7,)),
            DMA((7,)),
            DMA((4,)),
            DMA((chunk_count,)),
            DMA((chunk_count,)),
            DMA((chunk_count, 3)),
            DMA((chunk_count, 3)),
            DMA((chunk_count, 4)),
            DMA((chunk_count, 4)),
        ],
        compiler_params=pltpu.CompilerParams(collective_id=0, has_side_effects=True),
        name="weight_gather",
    )(pieces, normed)
    partial = pl.pallas_call(
        attention_kernel,
        out_shape=jax.ShapeDtypeStruct((2, row_count, model_width), jnp.float32),
        in_specs=[VMEM, VMEM],
        out_specs=VMEM,
        name="attention",
    )(weights, both)
    experts_here = lax.axis_size("expert")
    expert_ids = jnp.arange(experts_here, dtype=jnp.int32)
    named = routes[:, :, None] == expert_ids[None, None, :]
    chosen = jnp.any(named, axis=1)
    weight_of = jnp.sum(jnp.where(named, route_weights[:, :, None], 0.0), axis=1)
    counted = chosen.astype(jnp.bfloat16)
    earlier = (jnp.arange(row_count)[:, None] > jnp.arange(row_count)[None, :]).astype(jnp.bfloat16)
    position = jnp.dot(earlier, counted, preferred_element_type=jnp.float32)
    position = jnp.where(chosen, position, -1.0)
    table = jnp.stack([position.T, weight_of.T]).reshape(2, NY, NX, 2, row_count)
    by_row = table.transpose(1, 0, 2, 3, 4).reshape(NY, 16, row_count)
    by_column = table.transpose(2, 0, 1, 3, 4).reshape(NX, 16, row_count)
    info = jnp.stack([by_row, by_column])
    hbm = pl.BlockSpec(memory_space=pl.ANY)
    width = gate_weight.shape[2]
    blocks = (SLOTS, HALF)
    return pl.pallas_call(
        moe_kernel,
        out_shape=jax.ShapeDtypeStruct((row_count, model_width), jnp.bfloat16),
        in_specs=[VMEM, VMEM, VMEM, VMEM, hbm, hbm, hbm],
        out_specs=VMEM,
        scratch_shapes=[
            pltpu.VMEM((row_count, model_width), jnp.float32),
            pltpu.VMEM((row_count, model_width), jnp.float32),
            pltpu.VMEM((model_width, width), jnp.bfloat16),
            pltpu.VMEM((model_width, width), jnp.bfloat16),
            pltpu.VMEM((width, model_width), jnp.bfloat16),
            pltpu.VMEM((2, 4, 16, row_count), jnp.float32),
            pltpu.VMEM((2, 4, row_count, HALF), jnp.bfloat16),
            pltpu.VMEM((2, 4, 4, 2) + blocks, jnp.bfloat16),
            pltpu.VMEM((2, 4, 4, 2) + blocks, jnp.bfloat16),
            pltpu.VMEM((2, 4, 2) + blocks, jnp.bfloat16),
            pltpu.VMEM((2, 4, 4, 2) + blocks, jnp.bfloat16),
            pltpu.VMEM((2, 4, 2, 4) + blocks, jnp.bfloat16),
            pltpu.VMEM((2, 4, 2) + blocks, jnp.bfloat16),
            pltpu.VMEM((2, 4, row_count, HALF), jnp.bfloat16),
            pltpu.VMEM((2, 4, row_count, HALF), jnp.bfloat16),
            pltpu.VMEM((2, 2, 64, HALF), jnp.bfloat16),
            pltpu.VMEM((2, row_count, HALF), jnp.float32),
            DMA((SENDS,)),
            DMA((RECVS,)),
        ],
        compiler_params=pltpu.CompilerParams(collective_id=1, has_side_effects=True),
        name="experts",
    )(partial, tokens, expert_gain.reshape(1, model_width), info, gate_weight[0], up_weight[0], down_weight[0])


def solution(mesh):
    placed = (
        P(("fsdp", "expert"), None),
        P(),
        P(("fsdp", "expert"), None),
        P(("fsdp", "expert"), None),
        P(),
        P(("fsdp", "expert"), None),
        P(("fsdp", "expert"), None),
        P("expert", None, None),
        P("expert", None, None),
        P("expert", None, None),
    )
    return jax.shard_map(
        per_device,
        mesh=mesh,
        in_specs=placed,
        out_specs=P(("fsdp", "expert"), None),
        check_vma=False,
    )
```

```python
import math

import jax
import jax.numpy as jnp
from jax import lax
from jax.experimental import pallas as pl
from jax.experimental.pallas import tpu as pltpu
from jax.sharding import PartitionSpec as P

MESH = pl.DeviceIdType.MESH
HEAD_DIM = 128
NX, NY, NZ = 4, 4, 16
SLOTS = 32
HALF = 512
QKV = 3 * HEAD_DIM
KS = (0, 1, 3, 2)
SENDS, RECVS = 304, 323


def rms_scale(inputs, scale_gain):
    mean_square = jnp.mean(inputs * inputs, axis=-1, keepdims=True)
    return inputs * lax.rsqrt(mean_square + 1e-06) * scale_gain


def place():
    z = lax.axis_index("fsdp")
    e = lax.axis_index("expert")
    return (e // 2) % NX, e // (2 * NX), z, e % 2


def expert_at(x, y, core):
    return (y * NX + x) * 2 + core


def layer_kernel(
    tok_ref,
    gain_a_ref,
    ain_ref,
    aout_ref,
    gain_e_ref,
    routes_ref,
    rw_ref,
    wg_hbm,
    wu_hbm,
    wd_hbm,
    out_ref,
    cut_q,
    cut_o,
    ex_q,
    ex_o,
    gq,
    go,
    normed,
    part,
    swap,
    hidden,
    wg,
    wu,
    wd,
    info,
    ibuf,
    g,
    disp,
    r,
    res,
    cbuf,
    sbuf,
    f,
    own_sum,
    ss,
    rv,
):
    x, y, z, core = place()
    j = 2 * x + core
    lines = ((y, x), (x, y))

    def dev(color, dp=0, dd=0, to=None):
        p, d = lines[color]
        p, d = (p + dp + 4) % 4, (d + dd + 4) % 4
        to = core if to is None else to
        return {"expert": expert_at(d, p, to) if color == 0 else expert_at(p, d, to)}

    def up_z(dz):
        return {"fsdp": (z + dz + NZ) % NZ}

    def peer(d):
        return {"expert": y * 2 * NX + (j + d) % 8}

    sibling = {"expert": expert_at(x, y, 1 - core)}
    near = [s * d for d in (1, 2, 3, 4) for s in (1, -1)]
    barrier = pltpu.get_barrier_semaphore()
    partners = [up_z(d) for d in near]
    partners += [dev(0, dp=d, to=to) for d in (2, 1, -1) for to in (0, 1)]
    partners += [peer(d) for d in range(1, 8)]
    for ident in partners:
        pl.semaphore_signal(barrier, inc=1, device_id=ident, device_id_type=MESH)

    sent, bases = [], {}

    def base(name, width=1):
        if name not in bases:
            bases[name] = sum(w for _, w in bases.values()), width
        return bases[name][0]

    def send(src, dst, name, ident, width=1):
        at = base(name, width)
        copy = pltpu.make_async_remote_copy(
            src_ref=src,
            dst_ref=dst,
            send_sem=ss.at[len(sent)],
            recv_sem=rv.at[at + core if width == 2 else at],
            device_id=ident,
            device_id_type=MESH,
        )
        copy.start()
        sent.append(copy.wait_send)

    def local(src, dst, name):
        pltpu.make_async_copy(src, dst, rv.at[base(name)]).start()

    def arrive(dst, name, which=0):
        pltpu.make_async_copy(dst, dst, rv.at[base(name) + which]).wait()

    for h in range(8):
        for i in range(3):
            cut_q[h, :, i * 128 : (i + 1) * 128] = ain_ref[:, (8 * i + h) * 128 : (8 * i + h + 1) * 128]
        cut_o[h] = aout_ref[:, h * 128 : (h + 1) * 128]
    ex_q[j] = cut_q[j]
    ex_o[j] = cut_o[j]
    normed[core] = rms_scale(tok_ref[...].astype(jnp.float32), gain_a_ref[...]).astype(jnp.bfloat16)
    pl.semaphore_wait(barrier, len(partners))

    for d in (4, 3, 5, 2, 6, 1, 7):
        send(cut_q.at[(j + d) % 8], ex_q.at[j], ("ex_q", d), peer(d))
    for d in (4, 3, 5, 2, 6, 1, 7):
        send(cut_o.at[(j + d) % 8], ex_o.at[j], ("ex_o", d), peer(d))
    send(normed.at[core], normed.at[core], "normed", sibling)
    for source, place_in, name in ((wg_hbm, wg, "wg"), (wu_hbm, wu, "wu"), (wd_hbm, wd, "wd")):
        local(source, place_in, name)

    expert_ids = lax.broadcasted_iota(jnp.int32, (32, 128), 0)
    chosen = jnp.zeros((32, 128), jnp.float32)
    weight_of = jnp.zeros((32, 128), jnp.float32)
    for k in range(routes_ref.shape[0]):
        hit = routes_ref[k : k + 1, :] == expert_ids
        chosen = jnp.where(hit, 1.0, chosen)
        weight_of = jnp.where(hit, rw_ref[k : k + 1, :], weight_of)
    earlier = lax.broadcasted_iota(jnp.int32, (128, 128), 0) < lax.broadcasted_iota(jnp.int32, (128, 128), 1)
    slot_of = jnp.dot(
        chosen.astype(jnp.bfloat16),
        jnp.where(earlier, 1.0, 0.0).astype(jnp.bfloat16),
        preferred_element_type=jnp.float32,
    )
    slot_of = jnp.where(chosen > 0.0, slot_of, -1.0)
    for at, table in ((0, slot_of), (8, weight_of)):
        for i in range(4):
            info[0, i, at : at + 8] = table[8 * i : 8 * i + 8]
            for q in range(4):
                info[1, i, at + 2 * q : at + 2 * q + 2] = table[8 * q + 2 * i : 8 * q + 2 * i + 2]

    def join(ref):
        pieces = [ref[i].astype(jnp.float32) for i in range(8)]
        return jnp.concatenate(pieces, axis=0).astype(jnp.bfloat16)

    for d in (4, 3, 5, 2, 6, 1, 7):
        arrive(ex_q.at[(j + d) % 8], ("ex_q", d))
    gq[x, z, y] = join(ex_q)
    mine = gq.at[x, z, y]

    def second(color, s, zs):
        here = gq.at[x, zs, y]
        for dp in (2, 1, -1):
            send(here, here, ("p2", color, s, dp), dev(color, dp=dp))

    for d in near:
        color = 0 if d > 0 else 1
        send(mine, mine, ("z", color, abs(d)), up_z(d))
        if d == -1:
            second(0, 0, z)

    for d in (4, 3, 5, 2, 6, 1, 7):
        arrive(ex_o.at[(j + d) % 8], ("ex_o", d))
    go[x, z, y] = join(ex_o)
    for d in near:
        send(go.at[x, z, y], go.at[x, z, y], ("zo", 0 if d > 0 else 1, abs(d)), up_z(d))
    for color in range(2):
        p, d = lines[color]
        for k in (1, 3, 2):
            send(info.at[color, (p + k) % 4], ibuf.at[color, p], ("info", color, k), dev(color, dp=k))
        ibuf[color, p] = info[color, p]

    def chunks(s):
        found = []
        if s <= NZ // 2 - 1:
            found.append((0, (z - s + NZ) % NZ))
        if s >= 1:
            found.append((1, (z + s) % NZ))
        return found

    def passed_on(ref, kind, color, zs):
        here = ref.at[x, zs, y]
        for i in range(1, 4 + color):
            send(here, here, (kind, color, 4 + i), up_z(i if color == 0 else -i))

    def stage_z(s):
        for color, zs in chunks(s):
            arrive(gq.at[x, zs, y], ("z", color, s))
            if s == 4:
                passed_on(gq, "z", color, zs)
            second(color, s, zs)

    def row_of(color, zs, index):
        return gq.at[x, zs, index] if color == 0 else gq.at[index, zs, y]

    def block_of(color, zs, index):
        return gq.at[index, zs] if color == 0 else gq.at[:, zs, index]

    def half_of(color, zs, index, i):
        part = pl.ds(2 * i, 2)
        return gq.at[index, zs, part] if color == 0 else gq.at[part, zs, index]

    def stage_third(s):
        for color, zs in chunks(s):
            p, d = lines[color]
            for dp in (1, -1, 2):
                arrive(row_of(color, zs, (p - dp + 4) % 4), ("p2", color, s, dp))
            for dd in (1, -1):
                send(block_of(color, zs, d), block_of(color, zs, d), ("p3", color, s, dd), dev(color, dd=dd))

    def stage_half(s):
        for color, zs in chunks(s):
            p, d = lines[color]
            for dd in (1, -1):
                arrive(block_of(color, zs, (d - dd + 4) % 4), ("p3", color, s, dd))
            for i, dd in enumerate((1, -1)):
                half = half_of(color, zs, (d - dd + 4) % 4, i)
                send(half, half, ("p4", color, s, i), dev(color, dd=dd))

    def stage_end(s):
        for color, zs in chunks(s):
            p, d = lines[color]
            for i in range(2):
                arrive(half_of(color, zs, (d + 2) % 4, i), ("p4", color, s, i))

    def out_pass_on():
        for color in range(2):
            zs = (z - 4 + NZ) % NZ if color == 0 else (z + 4) % NZ
            arrive(go.at[x, zs, y], ("zo", color, 4))
            passed_on(go, "zo", color, zs)

    def out_row(color, index):
        zs = pl.ds(8 * color, 8)
        return go.at[x, zs, index] if color == 0 else go.at[index, zs, y]

    def out_block(color, index):
        zs = pl.ds(8 * color, 8)
        return go.at[index, zs] if color == 0 else go.at[:, zs, index]

    def out_half(color, index, i):
        zs, part = pl.ds(8 * color, 8), pl.ds(2 * i, 2)
        return go.at[index, zs, part] if color == 0 else go.at[part, zs, index]

    def out_second():
        for s in range(1, 9):
            for color, zs in chunks(s):
                if s != 4:
                    arrive(go.at[x, zs, y], ("zo", color, s))
        for color in range(2):
            p, d = lines[color]
            for dp in (2, 1, -1):
                send(out_row(color, p), out_row(color, p), ("o2", color, dp), dev(color, dp=dp))

    def out_third():
        for color in range(2):
            p, d = lines[color]
            for dp in (1, -1, 2):
                arrive(out_row(color, (p - dp + 4) % 4), ("o2", color, dp))
            for dd in (1, -1):
                send(out_block(color, d), out_block(color, d), ("o3", color, dd), dev(color, dd=dd))

    def out_halves():
        for color in range(2):
            p, d = lines[color]
            for dd in (1, -1):
                arrive(out_block(color, (d - dd + 4) % 4), ("o3", color, dd))
            for i, dd in enumerate((1, -1)):
                half = out_half(color, (d - dd + 4) % 4, i)
                send(half, half, ("o4", color, i), dev(color, dd=dd))

    def out_end():
        for color in range(2):
            p, d = lines[color]
            for i in range(2):
                arrive(out_half(color, (d + 2) % 4, i), ("o4", color, i))

    stage_z(1)
    stage_z(2)
    stage_third(0)
    stage_z(3)
    stage_z(4)
    out_pass_on()
    stage_third(1)
    stage_half(0)
    stage_third(2)
    stage_z(5)
    stage_third(3)
    stage_half(1)
    stage_z(6)
    stage_third(4)
    stage_z(7)
    stage_half(2)
    stage_z(8)
    stage_third(5)
    stage_half(3)
    stage_third(6)
    stage_half(4)
    out_second()
    stage_third(7)
    stage_half(5)
    stage_third(8)
    stage_half(6)
    stage_half(7)
    out_third()
    stage_half(8)
    for s in range(9):
        stage_end(s)

    arrive(normed.at[1 - core], "normed")
    rows = normed[...].reshape(256, 1024)
    causal = lax.broadcasted_iota(jnp.int32, (128, 128), 0) >= lax.broadcasted_iota(jnp.int32, (128, 128), 1)
    heads = [[], []]
    for h in range(NX):
        qkv = jnp.dot(rows, gq[h].reshape(1024, QKV), preferred_element_type=jnp.float32).astype(jnp.bfloat16)
        for s in range(2):
            piece = qkv[s * 128 : (s + 1) * 128]
            q, k, v = piece[:, 0:128], piece[:, 128:256], piece[:, 256:384]
            scores = lax.dot_general(
                q, k, (((1,), (1,)), ((), ())), preferred_element_type=jnp.float32
            ) / math.sqrt(HEAD_DIM)
            raised = jnp.where(causal, jnp.exp(jnp.where(causal, scores, 0.0)), 0.0)
            probs = (raised / jnp.sum(raised, axis=-1, keepdims=True)).astype(jnp.bfloat16)
            heads[s].append(jnp.dot(probs, v, preferred_element_type=jnp.float32).astype(jnp.bfloat16))
        if h == 0:
            out_halves()
    out_end()
    total = jnp.zeros((256, 1024), jnp.float32)
    for h in range(NX):
        both_rows = jnp.concatenate([heads[0][h], heads[1][h]], axis=0)
        total = total + lax.dot_general(
            both_rows, go[h].reshape(1024, 128), (((1,), (1,)), ((), ())), preferred_element_type=jnp.float32
        )
    part[0] = total[0:128]
    part[1] = total[128:256]
    send(part.at[1 - core], swap, "swap", sibling)
    stream = tok_ref[...].astype(jnp.float32) + part[core]
    arrive(swap, "swap")
    stream = stream + swap[...]
    hidden[...] = stream
    expert_in = rms_scale(stream, gain_e_ref[...]).astype(jnp.bfloat16)
    g[0, y] = expert_in[:, 0:HALF]
    g[1, x] = expert_in[:, HALF : 2 * HALF]

    for color in range(2):
        p, d = lines[color]
        for k in (1, 3):
            send(g.at[color, p], g.at[color, p], ("g", color, k), dev(color, dp=k))

    def first_near(color, k):
        p, d = lines[color]
        arrive(g.at[color, (p - k + 4) % 4], ("g", color, k))
        i = 0 if k == 1 else 1
        block = g.at[color, (p - k + 4) % 4, pl.ds(64 * i, 64)]
        send(block, block, ("g2", color, k), dev(color, dp=k))

    def first_last(color):
        p, d = lines[color]
        for i, k in enumerate((1, 3)):
            arrive(g.at[color, (p + 2) % 4, pl.ds(64 * i, 64)], ("g2", color, k))

    slot_ids = lax.broadcasted_iota(jnp.int32, (SLOTS, 128), 0).astype(jnp.float32)

    def spread(color, k, weighted):
        p, d = lines[color]
        table = ibuf[color, (p + k) % 4]
        blocks = []
        for i in range(8):
            hit = table[i : i + 1] == slot_ids
            blocks.append(jnp.where(hit, table[8 + i : 9 + i] if weighted else 1.0, 0.0))
        return jnp.concatenate(blocks, axis=0)

    def dispatch(color, k):
        p, d = lines[color]
        seq = (p + k) % 4
        rows = jnp.dot(
            spread(color, k, False).astype(jnp.bfloat16), g[color, seq], preferred_element_type=jnp.float32
        ).astype(jnp.bfloat16)
        disp[color, k] = rows.reshape(4, 2, SLOTS, HALF)
        target = r.at[color, d, seq, core]
        for dd in (2, 1, -1):
            for to in range(2):
                src = disp.at[color, k, (d + dd + 4) % 4, to]
                send(src, target, ("d", color, k, dd), dev(color, dd=dd, to=to), width=2)
        send(disp.at[color, k, d, 1 - core], target, ("d", color, k, 0), sibling)
        local(disp.at[color, k, d, core], target, ("d", color, k, "here"))

    def arrivals(kind, color, k, dd, block):
        if dd == 0:
            arrive(block(core), (kind, color, k, "here"))
            arrive(block(1 - core), (kind, color, k, 0))
            return
        for from_core in range(2):
            arrive(block(from_core), (kind, color, k, 2 if dd == 2 else -dd), from_core)

    def group(k):
        column = (x + k) % 4
        across = {0: 0, 1: 1, 3: -1, 2: 2}[k]
        for kk in KS:
            arrivals("d", 0, kk, across, lambda c: r.at[0, column, (y + kk) % 4, c])
        for dd in (0, 1, -1, 2):
            arrivals("d", 1, k, dd, lambda c: r.at[1, (y + dd + 4) % 4, column, c])
        low = r[0, column].reshape(256, HALF)
        high = r[1, :, pl.ds(column, 1)].reshape(256, HALF)

        def product(weight):
            by_row = (((1,), (1,)), ((), ()))
            return lax.dot_general(
                low, weight[:, 0:HALF], by_row, preferred_element_type=jnp.float32
            ) + lax.dot_general(high, weight[:, HALF : 2 * HALF], by_row, preferred_element_type=jnp.float32)

        gate, up = product(wg), product(wu)
        inner = (gate / (1.0 + jnp.exp(-gate)) * up).astype(jnp.bfloat16)
        result = jnp.dot(inner, wd[...], preferred_element_type=jnp.float32).astype(jnp.bfloat16)
        res[0, k] = result[:, 0:HALF].reshape(4, 2, SLOTS, HALF)
        res[1, k] = result[:, HALF : 2 * HALF].reshape(4, 2, SLOTS, HALF)
        pairs = [(1, k, dd) for dd in (2, 1, -1, 0)] + [(0, kk, across) for kk in (2, 1, 3, 0)]
        for color, kk, dd in pairs:
            p, d = lines[color]
            row = (y + kk) % 4 if color == 0 else (y + dd + 4) % 4
            target = cbuf.at[color, d, core, (p + kk) % 4]
            if dd == 0:
                send(res.at[color, k, row, 1 - core], target, ("r", color, kk, 0), sibling)
                local(res.at[color, k, row, core], target, ("r", color, kk, "here"))
            else:
                for to in range(2):
                    src = res.at[color, k, row, to]
                    send(src, target, ("r", color, kk, dd), dev(color, dd=dd, to=to), width=2)

    def combine(color, k):
        p, d = lines[color]
        seq = (p + k) % 4
        for dd in (0, 1, -1, 2):
            arrivals("r", color, k, dd, lambda c: cbuf.at[color, (d + dd + 4) % 4, c, seq])
        scale = spread(color, k, True)
        high = scale.astype(jnp.bfloat16)
        low = (scale - high.astype(jnp.float32)).astype(jnp.bfloat16)
        rows = cbuf[color, :, :, pl.ds(seq, 1)].reshape(256, HALF)
        total = 0.0
        for term in (high, low):
            total = total + lax.dot_general(
                term, rows, (((0,), (0,)), ((), ())), preferred_element_type=jnp.float32
            )
        if k == 0:
            own_sum[color] = total
            return
        sbuf[color, k] = total.astype(jnp.bfloat16)
        send(sbuf.at[color, k], f.at[color, k], ("f", color, k), dev(color, dp=k))

    both = (0, 1)
    for color in both:
        dispatch(color, 0)
    for color in both:
        for k in (1, 3, 2):
            arrive(ibuf.at[color, (lines[color][0] - k + 4) % 4], ("info", color, k))
    for k in (1, 3):
        for color in both:
            first_near(color, k)
    for k in (1, 3):
        for color in both:
            dispatch(color, (4 - k) % 4)
    for color in both:
        first_last(color)
        dispatch(color, 2)
    arrive(wg, "wg")
    arrive(wu, "wu")
    arrive(wd, "wd")
    group(0)
    group(1)
    combine(1, 0)
    group(3)
    combine(1, 1)
    group(2)
    combine(1, 3)
    combine(0, 2)
    combine(1, 2)
    combine(0, 1)
    combine(0, 3)
    combine(0, 0)
    for color in (1, 0):
        cols = pl.ds(HALF * color, HALF)
        total = hidden[:, cols] + own_sum[color]
        for k in (1, 3, 2):
            arrive(f.at[color, k], ("f", color, k))
            total = total + f[color, k].astype(jnp.float32)
        out_ref[:, cols] = total.astype(out_ref.dtype)
    for wait in sent:
        wait()


def per_device(
    tokens,
    attention_gain,
    attention_in,
    attention_out,
    expert_gain,
    routes,
    route_weights,
    gate_weight,
    up_weight,
    down_weight,
):
    rows, model = tokens.shape
    width = gate_weight.shape[2]
    vmem = pl.BlockSpec(memory_space=pltpu.VMEM)
    hbm = pl.BlockSpec(memory_space=pl.ANY)
    blocks = (SLOTS, HALF)
    scratch = [
        ((8, 2, QKV), jnp.bfloat16),
        ((8, 2, HEAD_DIM), jnp.bfloat16),
        ((8, 2, QKV), jnp.bfloat16),
        ((8, 2, HEAD_DIM), jnp.bfloat16),
        ((NX, NZ, NY, 16, QKV), jnp.bfloat16),
        ((NX, NZ, NY, 16, HEAD_DIM), jnp.bfloat16),
        ((2, rows, model), jnp.bfloat16),
        ((2, rows, model), jnp.float32),
        ((rows, model), jnp.float32),
        ((rows, model), jnp.float32),
        ((width, model), jnp.bfloat16),
        ((width, model), jnp.bfloat16),
        ((width, model), jnp.bfloat16),
        ((2, 4, 16, rows), jnp.float32),
        ((2, 4, 16, rows), jnp.float32),
        ((2, 4, rows, HALF), jnp.bfloat16),
        ((2, 4, 4, 2) + blocks, jnp.bfloat16),
        ((2, 4, 4, 2) + blocks, jnp.bfloat16),
        ((2, 4, 4, 2) + blocks, jnp.bfloat16),
        ((2, 4, 2, 4) + blocks, jnp.bfloat16),
        ((2, 4, rows, HALF), jnp.bfloat16),
        ((2, 4, rows, HALF), jnp.bfloat16),
        ((2, rows, HALF), jnp.float32),
    ]
    mixed = pl.pallas_call(
        layer_kernel,
        out_shape=jax.ShapeDtypeStruct((rows, model), jnp.bfloat16),
        in_specs=[vmem] * 7 + [hbm] * 3,
        out_specs=vmem,
        scratch_shapes=[pltpu.VMEM(shape, dtype) for shape, dtype in scratch]
        + [pltpu.SemaphoreType.DMA((SENDS,)), pltpu.SemaphoreType.DMA((RECVS,))],
        compiler_params=pltpu.CompilerParams(collective_id=0, has_side_effects=True),
        name="layer",
    )(
        tokens,
        attention_gain.reshape(1, model),
        attention_in,
        attention_out,
        expert_gain.reshape(1, model),
        routes.T,
        route_weights.T,
        gate_weight[0].T,
        up_weight[0].T,
        down_weight[0],
    )
    return mixed.astype(jnp.bfloat16)


def solution(mesh):
    placed = (
        P(("fsdp", "expert"), None),
        P(),
        P(("fsdp", "expert"), None),
        P(("fsdp", "expert"), None),
        P(),
        P(("fsdp", "expert"), None),
        P(("fsdp", "expert"), None),
        P("expert", None, None),
        P("expert", None, None),
        P("expert", None, None),
    )
    return jax.shard_map(
        per_device,
        mesh=mesh,
        in_specs=placed,
        out_specs=P(("fsdp", "expert"), None),
        check_vma=False,
    )
```

```python
import math

import jax
import jax.numpy as jnp
from jax import lax
from jax.experimental import pallas as pl
from jax.experimental.pallas import tpu as pltpu
from jax.sharding import PartitionSpec as P

MESH = pl.DeviceIdType.MESH
HEAD_DIM = 128
NX, NY, NZ = 4, 4, 16
SLOTS = 32
HALF = 512
QKV = 3 * HEAD_DIM
KS = (0, 1, 3, 2)
LATE = 7
SENDS, RECVS = 299, 325


def rms_scale(inputs, scale_gain):
    mean_square = jnp.mean(inputs * inputs, axis=-1, keepdims=True)
    return inputs * lax.rsqrt(mean_square + 1e-06) * scale_gain


def place():
    z = lax.axis_index("fsdp")
    e = lax.axis_index("expert")
    return (e // 2) % NX, e // (2 * NX), z, e % 2


def expert_at(x, y, core):
    return (y * NX + x) * 2 + core


def layer_kernel(
    tok_hbm,
    gain_a_hbm,
    ain_hbm,
    aout_hbm,
    gain_e_hbm,
    routes_hbm,
    rw_hbm,
    wg_hbm,
    wu_hbm,
    wd_hbm,
    out_ref,
    tok_ref,
    gain_a_ref,
    ain_ref,
    aout_ref,
    gain_e_ref,
    routes_ref,
    rw_ref,
    cut_q,
    cut_o,
    ex_q,
    ex_o,
    gq,
    go,
    normed,
    part,
    swap,
    hidden,
    wg,
    wu,
    wd,
    info,
    ibuf,
    g,
    disp,
    r,
    res,
    cbuf,
    sbuf,
    f,
    own_sum,
    ss,
    rv,
):
    x, y, z, core = place()
    j = 2 * x + core
    lines = ((y, x), (x, y))

    def dev(color, dp=0, dd=0, to=None):
        p, d = lines[color]
        p, d = (p + dp + 4) % 4, (d + dd + 4) % 4
        to = core if to is None else to
        return {"expert": expert_at(d, p, to) if color == 0 else expert_at(p, d, to)}

    def up_z(dz):
        return {"fsdp": (z + dz + NZ) % NZ}

    def peer(d):
        return {"expert": y * 2 * NX + (j + d) % 8}

    sibling = {"expert": expert_at(x, y, 1 - core)}
    near = [s * d for d in (4, 1, 2, 3) for s in (1, -1)]
    barrier = pltpu.get_barrier_semaphore()
    partners = [up_z(d) for d in near]
    partners += [dev(0, dp=d, to=to) for d in (2, 1, -1) for to in (0, 1)]
    partners += [peer(d) for d in range(1, 8)]
    for ident in partners:
        pl.semaphore_signal(barrier, inc=1, device_id=ident, device_id_type=MESH)

    sent, bases = [], {}

    def base(name, width=1):
        if name not in bases:
            bases[name] = sum(w for _, w in bases.values()), width
        return bases[name][0]

    def send(src, dst, name, ident, width=1):
        at = base(name, width)
        copy = pltpu.make_async_remote_copy(
            src_ref=src,
            dst_ref=dst,
            send_sem=ss.at[len(sent)],
            recv_sem=rv.at[at + core if width == 2 else at],
            device_id=ident,
            device_id_type=MESH,
        )
        copy.start()
        sent.append(copy.wait_send)

    drained = [0]

    def drain(upto):
        for wait in sent[drained[0] : upto]:
            wait()
        drained[0] = upto

    def local(src, dst, name):
        pltpu.make_async_copy(src, dst, rv.at[base(name)]).start()

    def arrive(dst, name, which=0):
        pltpu.make_async_copy(dst, dst, rv.at[base(name) + which]).wait()

    staged = (
        (ain_hbm, ain_ref, "ain"),
        (aout_hbm, aout_ref, "aout"),
        (tok_hbm, tok_ref, "tok"),
        (gain_a_hbm, gain_a_ref, "gain_a"),
        (routes_hbm, routes_ref, "routes"),
        (rw_hbm, rw_ref, "rw"),
        (gain_e_hbm, gain_e_ref, "gain_e"),
    )
    for source, place_in, name in staged:
        local(source, place_in, name)
    for _, place_in, name in staged[:2]:
        arrive(place_in, name)
    for h in range(8):
        for i in range(3):
            cut_q[h, :, i * 128 : (i + 1) * 128] = ain_ref[:, (8 * i + h) * 128 : (8 * i + h + 1) * 128]
        cut_o[h] = aout_ref[:, h * 128 : (h + 1) * 128]
    ex_q[j] = cut_q[j]
    ex_o[j] = cut_o[j]
    pl.semaphore_wait(barrier, len(partners))

    for d in (4, 3, 5, 2, 6, 1, 7):
        send(cut_q.at[(j + d) % 8], ex_q.at[j], ("ex_q", d), peer(d))
    for d in (4, 3, 5, 2, 6, 1, 7):
        send(cut_o.at[(j + d) % 8], ex_o.at[j], ("ex_o", d), peer(d))
    for _, place_in, name in staged[2:]:
        arrive(place_in, name)
    normed[core] = rms_scale(tok_ref[...].astype(jnp.float32), gain_a_ref[...]).astype(jnp.bfloat16)
    send(normed.at[core], normed.at[core], "normed", sibling)
    for source, place_in, name in ((wg_hbm, wg, "wg"), (wu_hbm, wu, "wu"), (wd_hbm, wd, "wd")):
        local(source, place_in, name)

    expert_ids = lax.broadcasted_iota(jnp.int32, (32, 128), 0)
    chosen = jnp.zeros((32, 128), jnp.float32)
    weight_of = jnp.zeros((32, 128), jnp.float32)
    for k in range(routes_ref.shape[0]):
        hit = routes_ref[k : k + 1, :] == expert_ids
        chosen = jnp.where(hit, 1.0, chosen)
        weight_of = jnp.where(hit, rw_ref[k : k + 1, :], weight_of)
    earlier = lax.broadcasted_iota(jnp.int32, (128, 128), 0) < lax.broadcasted_iota(jnp.int32, (128, 128), 1)
    slot_of = jnp.dot(
        chosen.astype(jnp.bfloat16),
        jnp.where(earlier, 1.0, 0.0).astype(jnp.bfloat16),
        preferred_element_type=jnp.float32,
    )
    slot_of = jnp.where(chosen > 0.0, slot_of, -1.0)
    for at, table in ((0, slot_of), (8, weight_of)):
        for i in range(4):
            info[0, i, at : at + 8] = table[8 * i : 8 * i + 8]
            for q in range(4):
                info[1, i, at + 2 * q : at + 2 * q + 2] = table[8 * q + 2 * i : 8 * q + 2 * i + 2]

    def join(ref):
        pieces = [ref[i].astype(jnp.float32) for i in range(8)]
        return jnp.concatenate(pieces, axis=0).astype(jnp.bfloat16)

    for d in (4, 3, 5, 2, 6, 1, 7):
        arrive(ex_q.at[(j + d) % 8], ("ex_q", d))
    gq[x, z, y] = join(ex_q)
    mine = gq.at[x, z, y]

    def second(color, s, zs):
        here = gq.at[x, zs, y]
        for dp in (2, 1, -1):
            send(here, here, ("p2", color, s, dp), dev(color, dp=dp))

    for d in near:
        color = 0 if d > 0 else 1
        send(mine, mine, ("z", color, abs(d)), up_z(d))
        if d == -4:
            second(0, 0, z)

    for d in (4, 3, 5, 2, 6, 1, 7):
        arrive(ex_o.at[(j + d) % 8], ("ex_o", d))
    go[x, z, y] = join(ex_o)
    for d in near:
        send(go.at[x, z, y], go.at[x, z, y], ("zo", 0 if d > 0 else 1, abs(d)), up_z(d))
    for color in range(2):
        p, d = lines[color]
        for k in (1, 3, 2):
            send(info.at[color, (p + k) % 4], ibuf.at[color, p], ("info", color, k), dev(color, dp=k))
        ibuf[color, p] = info[color, p]

    def chunks(s):
        found = []
        if s <= NZ // 2 - 1:
            found.append((0, (z - s + NZ) % NZ))
        if s >= 1:
            found.append((1, (z + s) % NZ))
        return found

    def passed_on(ref, kind, color, zs):
        here = ref.at[x, zs, y]
        for i in range(3 + color, 0, -1):
            send(here, here, (kind, color, 4 + i), up_z(i if color == 0 else -i))

    def stage_z(s):
        for color, zs in chunks(s):
            arrive(gq.at[x, zs, y], ("z", color, s))
            if s == 4:
                passed_on(gq, "z", color, zs)
            second(color, s, zs)

    def row_of(color, zs, index):
        return gq.at[x, zs, index] if color == 0 else gq.at[index, zs, y]

    def block_of(color, zs, index):
        return gq.at[index, zs] if color == 0 else gq.at[:, zs, index]

    def half_of(color, zs, index, i):
        part = pl.ds(2 * i, 2)
        return gq.at[index, zs, part] if color == 0 else gq.at[part, zs, index]

    def stage_third(s):
        for color, zs in chunks(s):
            p, d = lines[color]
            for dp in (1, -1, 2):
                arrive(row_of(color, zs, (p - dp + 4) % 4), ("p2", color, s, dp))
            for dd in (1, -1) if s < LATE else (2, 1, -1):
                send(block_of(color, zs, d), block_of(color, zs, d), ("p3", color, s, dd), dev(color, dd=dd))

    def stage_half(s):
        for color, zs in chunks(s):
            p, d = lines[color]
            for dd in (1, -1):
                arrive(block_of(color, zs, (d - dd + 4) % 4), ("p3", color, s, dd))
            for i, dd in enumerate((1, -1)):
                half = half_of(color, zs, (d - dd + 4) % 4, i)
                send(half, half, ("p4", color, s, i), dev(color, dd=dd))

    def stage_end(s):
        for color, zs in chunks(s):
            p, d = lines[color]
            if s >= LATE:
                for dd in (1, -1, 2):
                    arrive(block_of(color, zs, (d - dd + 4) % 4), ("p3", color, s, dd))
                continue
            for i in range(2):
                arrive(half_of(color, zs, (d + 2) % 4, i), ("p4", color, s, i))

    def out_pass_on():
        for color in range(2):
            zs = (z - 4 + NZ) % NZ if color == 0 else (z + 4) % NZ
            arrive(go.at[x, zs, y], ("zo", color, 4))
            passed_on(go, "zo", color, zs)

    def out_row(color, index):
        zs = pl.ds(8 * color, 8)
        return go.at[x, zs, index] if color == 0 else go.at[index, zs, y]

    def out_block(color, index):
        zs = pl.ds(8 * color, 8)
        return go.at[index, zs] if color == 0 else go.at[:, zs, index]

    def out_second():
        for s in range(1, 9):
            for color, zs in chunks(s):
                if s != 4:
                    arrive(go.at[x, zs, y], ("zo", color, s))
        for color in range(2):
            p, d = lines[color]
            for dp in (2, 1, -1):
                send(out_row(color, p), out_row(color, p), ("o2", color, dp), dev(color, dp=dp))

    def out_third():
        for color in range(2):
            p, d = lines[color]
            for dp in (1, -1, 2):
                arrive(out_row(color, (p - dp + 4) % 4), ("o2", color, dp))
            for dd in (2, 1, -1):
                send(out_block(color, d), out_block(color, d), ("o3", color, dd), dev(color, dd=dd))

    def out_end():
        for color in range(2):
            p, d = lines[color]
            for dd in (1, -1, 2):
                arrive(out_block(color, (d - dd + 4) % 4), ("o3", color, dd))

    stage_z(1)
    stage_z(2)
    stage_z(3)
    stage_z(4)
    stage_third(0)
    out_pass_on()
    stage_third(1)
    stage_third(2)
    stage_z(5)
    stage_third(3)
    stage_half(0)
    stage_third(4)
    stage_z(6)
    stage_z(7)
    stage_z(8)
    out_second()
    stage_half(1)
    stage_third(5)
    stage_half(2)
    stage_third(6)
    stage_third(7)
    stage_half(3)
    stage_third(8)
    stage_half(4)
    stage_half(5)
    stage_half(6)
    out_third()
    for s in range(9):
        stage_end(s)

    before_attention = len(sent)
    arrive(normed.at[1 - core], "normed")
    rows = normed[...].reshape(256, 1024)
    causal = lax.broadcasted_iota(jnp.int32, (128, 128), 0) >= lax.broadcasted_iota(jnp.int32, (128, 128), 1)
    heads = [[], []]
    for h in range(NX):
        qkv = jnp.dot(rows, gq[h].reshape(1024, QKV), preferred_element_type=jnp.float32).astype(jnp.bfloat16)
        for s in range(2):
            piece = qkv[s * 128 : (s + 1) * 128]
            q, k, v = piece[:, 0:128], piece[:, 128:256], piece[:, 256:384]
            scores = lax.dot_general(
                q, k, (((1,), (1,)), ((), ())), preferred_element_type=jnp.float32
            ) / math.sqrt(HEAD_DIM)
            raised = jnp.where(causal, jnp.exp(jnp.where(causal, scores, 0.0)), 0.0)
            probs = (raised / jnp.sum(raised, axis=-1, keepdims=True)).astype(jnp.bfloat16)
            heads[s].append(jnp.dot(probs, v, preferred_element_type=jnp.float32).astype(jnp.bfloat16))
    out_end()
    wide = [jnp.concatenate(heads[i], axis=1) for i in range(2)]
    mine_first = core == 0
    other_heads = jnp.where(mine_first, wide[1], wide[0])
    own_heads = jnp.where(mine_first, wide[0], wide[1])

    def project(rows_in):
        total = jnp.zeros((128, 1024), jnp.float32)
        for h in range(NX):
            total = total + lax.dot_general(
                rows_in[:, h * 128 : (h + 1) * 128],
                go[h].reshape(1024, 128),
                (((1,), (1,)), ((), ())),
                preferred_element_type=jnp.float32,
            )
        return total

    part[...] = project(other_heads).astype(jnp.bfloat16)
    send(part, swap, "swap", sibling)
    stream = tok_ref[...].astype(jnp.float32) + project(own_heads)
    drain(before_attention)
    arrive(swap, "swap")
    stream = stream + swap[...].astype(jnp.float32)
    hidden[...] = stream
    expert_in = rms_scale(stream, gain_e_ref[...]).astype(jnp.bfloat16)
    g[0, y] = expert_in[:, 0:HALF]
    g[1, x] = expert_in[:, HALF : 2 * HALF]

    for color in range(2):
        p, d = lines[color]
        for k in (1, 3):
            send(g.at[color, p], g.at[color, p], ("g", color, k), dev(color, dp=k))

    def first_near(color, k):
        p, d = lines[color]
        arrive(g.at[color, (p - k + 4) % 4], ("g", color, k))
        i = 0 if k == 1 else 1
        block = g.at[color, (p - k + 4) % 4, pl.ds(64 * i, 64)]
        send(block, block, ("g2", color, k), dev(color, dp=k))

    def first_last(color):
        p, d = lines[color]
        for i, k in enumerate((1, 3)):
            arrive(g.at[color, (p + 2) % 4, pl.ds(64 * i, 64)], ("g2", color, k))

    slot_ids = lax.broadcasted_iota(jnp.int32, (SLOTS, 128), 0).astype(jnp.float32)

    def spread(color, k, weighted):
        p, d = lines[color]
        table = ibuf[color, (p + k) % 4]
        blocks = []
        for i in range(8):
            hit = table[i : i + 1] == slot_ids
            blocks.append(jnp.where(hit, table[8 + i : 9 + i] if weighted else 1.0, 0.0))
        return jnp.concatenate(blocks, axis=0)

    def dispatch(color, k):
        p, d = lines[color]
        seq = (p + k) % 4
        rows = jnp.dot(
            spread(color, k, False).astype(jnp.bfloat16), g[color, seq], preferred_element_type=jnp.float32
        ).astype(jnp.bfloat16)
        disp[color, k] = rows.reshape(4, 2, SLOTS, HALF)
        target = r.at[color, d, seq, core]
        for dd in (2, 1, -1):
            for to in range(2):
                src = disp.at[color, k, (d + dd + 4) % 4, to]
                send(src, target, ("d", color, k, dd), dev(color, dd=dd, to=to), width=2)
        send(disp.at[color, k, d, 1 - core], target, ("d", color, k, 0), sibling)
        local(disp.at[color, k, d, core], target, ("d", color, k, "here"))

    def arrivals(kind, color, k, dd, block):
        if dd == 0:
            arrive(block(core), (kind, color, k, "here"))
            arrive(block(1 - core), (kind, color, k, 0))
            return
        for from_core in range(2):
            arrive(block(from_core), (kind, color, k, 2 if dd == 2 else -dd), from_core)

    def group(k):
        column = (x + k) % 4
        across = {0: 0, 1: 1, 3: -1, 2: 2}[k]
        for kk in KS:
            arrivals("d", 0, kk, across, lambda c: r.at[0, column, (y + kk) % 4, c])
        for dd in (0, 1, -1, 2):
            arrivals("d", 1, k, dd, lambda c: r.at[1, (y + dd + 4) % 4, column, c])
        low = r[0, column].reshape(256, HALF)
        high = r[1, :, pl.ds(column, 1)].reshape(256, HALF)

        def product(weight):
            by_row = (((1,), (1,)), ((), ()))
            return lax.dot_general(
                low, weight[:, 0:HALF], by_row, preferred_element_type=jnp.float32
            ) + lax.dot_general(high, weight[:, HALF : 2 * HALF], by_row, preferred_element_type=jnp.float32)

        gate, up = product(wg), product(wu)
        inner = (gate / (1.0 + jnp.exp(-gate)) * up).astype(jnp.bfloat16)
        result = jnp.dot(inner, wd[...], preferred_element_type=jnp.float32).astype(jnp.bfloat16)
        res[0, k] = result[:, 0:HALF].reshape(4, 2, SLOTS, HALF)
        res[1, k] = result[:, HALF : 2 * HALF].reshape(4, 2, SLOTS, HALF)
        pairs = [(1, k, dd) for dd in (2, 1, -1, 0)] + [(0, kk, across) for kk in (2, 1, 3, 0)]
        for color, kk, dd in pairs:
            p, d = lines[color]
            row = (y + kk) % 4 if color == 0 else (y + dd + 4) % 4
            target = cbuf.at[color, d, core, (p + kk) % 4]
            if dd == 0:
                send(res.at[color, k, row, 1 - core], target, ("r", color, kk, 0), sibling)
                local(res.at[color, k, row, core], target, ("r", color, kk, "here"))
            else:
                for to in range(2):
                    src = res.at[color, k, row, to]
                    send(src, target, ("r", color, kk, dd), dev(color, dd=dd, to=to), width=2)

    def combine(color, k):
        p, d = lines[color]
        seq = (p + k) % 4
        for dd in (0, 1, -1, 2):
            arrivals("r", color, k, dd, lambda c: cbuf.at[color, (d + dd + 4) % 4, c, seq])
        scale = spread(color, k, True)
        high = scale.astype(jnp.bfloat16)
        low = (scale - high.astype(jnp.float32)).astype(jnp.bfloat16)
        rows = cbuf[color, :, :, pl.ds(seq, 1)].reshape(256, HALF)
        total = 0.0
        for term in (high, low):
            total = total + lax.dot_general(
                term, rows, (((0,), (0,)), ((), ())), preferred_element_type=jnp.float32
            )
        if k == 0:
            own_sum[color] = total
            return
        sbuf[color, k] = total.astype(jnp.bfloat16)
        send(sbuf.at[color, k], f.at[color, k], ("f", color, k), dev(color, dp=k))

    both = (0, 1)
    for color in both:
        dispatch(color, 0)
    for color in both:
        for k in (1, 3, 2):
            arrive(ibuf.at[color, (lines[color][0] - k + 4) % 4], ("info", color, k))
    for k in (1, 3):
        for color in both:
            first_near(color, k)
    for k in (1, 3):
        for color in both:
            dispatch(color, (4 - k) % 4)
    for color in both:
        first_last(color)
        dispatch(color, 2)
    before_groups = len(sent)
    arrive(wg, "wg")
    arrive(wu, "wu")
    arrive(wd, "wd")
    group(0)
    group(1)
    combine(1, 0)
    group(3)
    combine(1, 1)
    group(2)
    combine(1, 3)
    drain(before_groups)
    combine(0, 2)
    combine(1, 2)
    combine(0, 1)
    combine(0, 3)
    combine(0, 0)
    for color in (1, 0):
        cols = pl.ds(HALF * color, HALF)
        total = hidden[:, cols] + own_sum[color]
        for k in (1, 3, 2):
            arrive(f.at[color, k], ("f", color, k))
            total = total + f[color, k].astype(jnp.float32)
        out_ref[:, cols] = total.astype(out_ref.dtype)
    drain(len(sent))


def per_device(
    tokens,
    attention_gain,
    attention_in,
    attention_out,
    expert_gain,
    routes,
    route_weights,
    gate_weight,
    up_weight,
    down_weight,
):
    rows, model = tokens.shape
    width = gate_weight.shape[2]
    vmem = pl.BlockSpec(memory_space=pltpu.VMEM)
    hbm = pl.BlockSpec(memory_space=pl.ANY)
    blocks = (SLOTS, HALF)
    scratch = [
        (tokens.shape, jnp.bfloat16),
        ((1, model), jnp.float32),
        (attention_in.shape, jnp.bfloat16),
        (attention_out.shape, jnp.bfloat16),
        ((1, model), jnp.float32),
        (routes.shape[::-1], jnp.int32),
        (routes.shape[::-1], jnp.float32),
        ((8, 2, QKV), jnp.bfloat16),
        ((8, 2, HEAD_DIM), jnp.bfloat16),
        ((8, 2, QKV), jnp.bfloat16),
        ((8, 2, HEAD_DIM), jnp.bfloat16),
        ((NX, NZ, NY, 16, QKV), jnp.bfloat16),
        ((NX, NZ, NY, 16, HEAD_DIM), jnp.bfloat16),
        ((2, rows, model), jnp.bfloat16),
        ((rows, model), jnp.bfloat16),
        ((rows, model), jnp.bfloat16),
        ((rows, model), jnp.float32),
        ((width, model), jnp.bfloat16),
        ((width, model), jnp.bfloat16),
        ((width, model), jnp.bfloat16),
        ((2, 4, 16, rows), jnp.float32),
        ((2, 4, 16, rows), jnp.float32),
        ((2, 4, rows, HALF), jnp.bfloat16),
        ((2, 4, 4, 2) + blocks, jnp.bfloat16),
        ((2, 4, 4, 2) + blocks, jnp.bfloat16),
        ((2, 4, 4, 2) + blocks, jnp.bfloat16),
        ((2, 4, 2, 4) + blocks, jnp.bfloat16),
        ((2, 4, rows, HALF), jnp.bfloat16),
        ((2, 4, rows, HALF), jnp.bfloat16),
        ((2, rows, HALF), jnp.float32),
    ]
    mixed = pl.pallas_call(
        layer_kernel,
        out_shape=jax.ShapeDtypeStruct((rows, model), jnp.bfloat16),
        in_specs=[hbm] * 10,
        out_specs=vmem,
        scratch_shapes=[pltpu.VMEM(shape, dtype) for shape, dtype in scratch]
        + [pltpu.SemaphoreType.DMA((SENDS,)), pltpu.SemaphoreType.DMA((RECVS,))],
        compiler_params=pltpu.CompilerParams(collective_id=0, has_side_effects=True),
        name="layer",
    )(
        tokens,
        attention_gain.reshape(1, model),
        attention_in,
        attention_out,
        expert_gain.reshape(1, model),
        routes.T,
        route_weights.T,
        gate_weight[0].T,
        up_weight[0].T,
        down_weight[0],
    )
    return mixed.astype(jnp.bfloat16)


def solution(mesh):
    placed = (
        P(("fsdp", "expert"), None),
        P(),
        P(("fsdp", "expert"), None),
        P(("fsdp", "expert"), None),
        P(),
        P(("fsdp", "expert"), None),
        P(("fsdp", "expert"), None),
        P("expert", None, None),
        P("expert", None, None),
        P("expert", None, None),
    )
    return jax.shard_map(
        per_device,
        mesh=mesh,
        in_specs=placed,
        out_specs=P(("fsdp", "expert"), None),
        check_vma=False,
    )
```

```python
import math

import jax
import jax.numpy as jnp
from jax import lax
from jax.experimental import pallas as pl
from jax.experimental.pallas import tpu as pltpu
from jax.sharding import PartitionSpec as P

MESH = pl.DeviceIdType.MESH
HEAD_DIM = 128
NX, NY, NZ = 4, 4, 16
SLOTS = 32
HALF = 512
QKV = 3 * HEAD_DIM
STEP = {0: 0, 1: 1, 3: -1, 2: 2}
LATE = 7
SENDS, RECVS = 299, 325


def rms_scale(inputs, scale_gain):
    mean_square = jnp.mean(inputs * inputs, axis=-1, keepdims=True)
    return inputs * lax.rsqrt(mean_square + 1e-06) * scale_gain


def place():
    z = lax.axis_index("fsdp")
    e = lax.axis_index("expert")
    return (e // 2) % NX, e // (2 * NX), z, e % 2


def expert_at(x, y, core):
    return (y * NX + x) * 2 + core


def layer_kernel(
    tok_hbm,
    gain_a_hbm,
    ain_hbm,
    aout_hbm,
    gain_e_hbm,
    routes_hbm,
    rw_hbm,
    wg_hbm,
    wu_hbm,
    wd_hbm,
    out_ref,
    tok_ref,
    gain_a_ref,
    ain_ref,
    aout_ref,
    gain_e_ref,
    routes_ref,
    rw_ref,
    cut_q,
    cut_o,
    ex_q,
    ex_o,
    gq,
    go,
    normed,
    part,
    swap,
    hidden,
    wg,
    wu,
    wd,
    info,
    ibuf,
    g,
    disp,
    r,
    res,
    cbuf,
    sbuf,
    f,
    own_sum,
    ss,
    rv,
):
    x, y, z, core = place()
    j = 2 * x + core
    lines = ((y, x), (x, y))

    def dev(color, dp=0, dd=0, to=None):
        p, d = lines[color]
        p, d = (p + dp + 4) % 4, (d + dd + 4) % 4
        to = core if to is None else to
        return {"expert": expert_at(d, p, to) if color == 0 else expert_at(p, d, to)}

    def up_z(dz):
        return {"fsdp": (z + dz + NZ) % NZ}

    def peer(d):
        return {"expert": y * 2 * NX + (j + d) % 8}

    sibling = {"expert": expert_at(x, y, 1 - core)}
    near = [s * d for d in (4, 1, 2, 3) for s in (1, -1)]
    barrier = pltpu.get_barrier_semaphore()
    partners = [up_z(d) for d in near]
    partners += [dev(0, dp=d, to=to) for d in (2, 1, -1) for to in (0, 1)]
    partners += [peer(d) for d in range(1, 8)]
    for ident in partners:
        pl.semaphore_signal(barrier, inc=1, device_id=ident, device_id_type=MESH)

    sent, bases = [], {}

    def base(name, width=1):
        if name not in bases:
            bases[name] = sum(w for _, w in bases.values()), width
        return bases[name][0]

    def send(src, dst, name, ident, width=1):
        at = base(name, width)
        copy = pltpu.make_async_remote_copy(
            src_ref=src,
            dst_ref=dst,
            send_sem=ss.at[len(sent)],
            recv_sem=rv.at[at + core if width == 2 else at],
            device_id=ident,
            device_id_type=MESH,
        )
        copy.start()
        sent.append(copy.wait_send)

    drained = [0]

    def drain(upto):
        for wait in sent[drained[0] : upto]:
            wait()
        drained[0] = upto

    def local(src, dst, name):
        pltpu.make_async_copy(src, dst, rv.at[base(name)]).start()

    def arrive(dst, name, which=0):
        pltpu.make_async_copy(dst, dst, rv.at[base(name) + which]).wait()

    staged = (
        (ain_hbm, ain_ref, "ain"),
        (aout_hbm, aout_ref, "aout"),
        (tok_hbm, tok_ref, "tok"),
        (gain_a_hbm, gain_a_ref, "gain_a"),
        (routes_hbm, routes_ref, "routes"),
        (rw_hbm, rw_ref, "rw"),
        (gain_e_hbm, gain_e_ref, "gain_e"),
    )
    for source, place_in, name in staged:
        local(source, place_in, name)
    for _, place_in, name in staged[:2]:
        arrive(place_in, name)
    for h in range(8):
        for i in range(3):
            cut_q[h, :, i * 128 : (i + 1) * 128] = ain_ref[:, (8 * i + h) * 128 : (8 * i + h + 1) * 128]
        cut_o[h] = aout_ref[:, h * 128 : (h + 1) * 128]
    ex_q[j] = cut_q[j]
    ex_o[j] = cut_o[j]
    pl.semaphore_wait(barrier, len(partners))

    for d in (4, 3, 5, 2, 6, 1, 7):
        send(cut_q.at[(j + d) % 8], ex_q.at[j], ("ex_q", d), peer(d))
    for d in (4, 3, 5, 2, 6, 1, 7):
        send(cut_o.at[(j + d) % 8], ex_o.at[j], ("ex_o", d), peer(d))
    for _, place_in, name in staged[2:]:
        arrive(place_in, name)
    normed[core] = rms_scale(tok_ref[...].astype(jnp.float32), gain_a_ref[...]).astype(jnp.bfloat16)
    send(normed.at[core], normed.at[core], "normed", sibling)
    for source, place_in, name in ((wg_hbm, wg, "wg"), (wu_hbm, wu, "wu"), (wd_hbm, wd, "wd")):
        local(source, place_in, name)

    expert_ids = lax.broadcasted_iota(jnp.int32, (32, 128), 0)
    chosen = jnp.zeros((32, 128), jnp.float32)
    weight_of = jnp.zeros((32, 128), jnp.float32)
    for k in range(routes_ref.shape[0]):
        hit = routes_ref[k : k + 1, :] == expert_ids
        chosen = jnp.where(hit, 1.0, chosen)
        weight_of = jnp.where(hit, rw_ref[k : k + 1, :], weight_of)
    earlier = lax.broadcasted_iota(jnp.int32, (128, 128), 0) < lax.broadcasted_iota(jnp.int32, (128, 128), 1)
    slot_of = jnp.dot(
        chosen.astype(jnp.bfloat16),
        jnp.where(earlier, 1.0, 0.0).astype(jnp.bfloat16),
        preferred_element_type=jnp.float32,
    )
    slot_of = jnp.where(chosen > 0.0, slot_of, -1.0)
    for at, table in ((0, slot_of), (8, weight_of)):
        for i in range(4):
            info[0, i, at : at + 8] = table[8 * i : 8 * i + 8]
            for q in range(4):
                info[1, i, at + 2 * q : at + 2 * q + 2] = table[8 * q + 2 * i : 8 * q + 2 * i + 2]

    def join(ref):
        pieces = [ref[i].astype(jnp.float32) for i in range(8)]
        return jnp.concatenate(pieces, axis=0).astype(jnp.bfloat16)

    for d in (4, 3, 5, 2, 6, 1, 7):
        arrive(ex_q.at[(j + d) % 8], ("ex_q", d))
    gq[x, z, y] = join(ex_q)
    mine = gq.at[x, z, y]

    def second(color, s, zs):
        here = gq.at[x, zs, y]
        for dp in (2, 1, -1):
            send(here, here, ("p2", color, s, dp), dev(color, dp=dp))

    for d in near:
        color = 0 if d > 0 else 1
        send(mine, mine, ("z", color, abs(d)), up_z(d))
        if d == -4:
            second(0, 0, z)

    for d in (4, 3, 5, 2, 6, 1, 7):
        arrive(ex_o.at[(j + d) % 8], ("ex_o", d))
    go[x, z, y] = join(ex_o)
    for d in near:
        send(go.at[x, z, y], go.at[x, z, y], ("zo", 0 if d > 0 else 1, abs(d)), up_z(d))
    for color in range(2):
        p, d = lines[color]
        for k in (1, 3, 2):
            send(info.at[color, (p + k) % 4], ibuf.at[color, p], ("info", color, k), dev(color, dp=k))
        ibuf[color, p] = info[color, p]

    def chunks(s):
        found = []
        if s <= NZ // 2 - 1:
            found.append((0, (z - s + NZ) % NZ))
        if s >= 1:
            found.append((1, (z + s) % NZ))
        return found

    def passed_on(ref, kind, color, zs):
        here = ref.at[x, zs, y]
        for i in range(3 + color, 0, -1):
            send(here, here, (kind, color, 4 + i), up_z(i if color == 0 else -i))

    def stage_z(s):
        for color, zs in chunks(s):
            arrive(gq.at[x, zs, y], ("z", color, s))
            if s == 4:
                passed_on(gq, "z", color, zs)
            second(color, s, zs)

    def row_of(color, zs, index):
        return gq.at[x, zs, index] if color == 0 else gq.at[index, zs, y]

    def block_of(color, zs, index):
        return gq.at[index, zs] if color == 0 else gq.at[:, zs, index]

    def half_of(color, zs, index, i):
        part = pl.ds(2 * i, 2)
        return gq.at[index, zs, part] if color == 0 else gq.at[part, zs, index]

    def stage_third(s):
        for color, zs in chunks(s):
            p, d = lines[color]
            for dp in (1, -1, 2):
                arrive(row_of(color, zs, (p - dp + 4) % 4), ("p2", color, s, dp))
            for dd in (1, -1) if s < LATE else (2, 1, -1):
                send(block_of(color, zs, d), block_of(color, zs, d), ("p3", color, s, dd), dev(color, dd=dd))

    def stage_half(s):
        for color, zs in chunks(s):
            p, d = lines[color]
            for dd in (1, -1):
                arrive(block_of(color, zs, (d - dd + 4) % 4), ("p3", color, s, dd))
            for i, dd in enumerate((1, -1)):
                half = half_of(color, zs, (d - dd + 4) % 4, i)
                send(half, half, ("p4", color, s, i), dev(color, dd=dd))

    def stage_end(s):
        for color, zs in chunks(s):
            p, d = lines[color]
            if s >= LATE:
                for dd in (1, -1, 2):
                    arrive(block_of(color, zs, (d - dd + 4) % 4), ("p3", color, s, dd))
                continue
            for i in range(2):
                arrive(half_of(color, zs, (d + 2) % 4, i), ("p4", color, s, i))

    def out_pass_on():
        for color in range(2):
            zs = (z - 4 + NZ) % NZ if color == 0 else (z + 4) % NZ
            arrive(go.at[x, zs, y], ("zo", color, 4))
            passed_on(go, "zo", color, zs)

    def out_row(color, index):
        zs = pl.ds(8 * color, 8)
        return go.at[x, zs, index] if color == 0 else go.at[index, zs, y]

    def out_block(color, index):
        zs = pl.ds(8 * color, 8)
        return go.at[index, zs] if color == 0 else go.at[:, zs, index]

    def out_second():
        for s in range(1, 9):
            for color, zs in chunks(s):
                if s != 4:
                    arrive(go.at[x, zs, y], ("zo", color, s))
        for color in range(2):
            p, d = lines[color]
            for dp in (2, 1, -1):
                send(out_row(color, p), out_row(color, p), ("o2", color, dp), dev(color, dp=dp))

    def out_third():
        for color in range(2):
            p, d = lines[color]
            for dp in (1, -1, 2):
                arrive(out_row(color, (p - dp + 4) % 4), ("o2", color, dp))
            for dd in (2, 1, -1):
                send(out_block(color, d), out_block(color, d), ("o3", color, dd), dev(color, dd=dd))

    def out_end():
        for color in range(2):
            p, d = lines[color]
            for dd in (1, -1, 2):
                arrive(out_block(color, (d - dd + 4) % 4), ("o3", color, dd))

    stage_z(1)
    stage_z(2)
    stage_z(3)
    stage_z(4)
    stage_third(0)
    out_pass_on()
    stage_third(1)
    stage_third(2)
    stage_z(5)
    stage_third(3)
    stage_half(0)
    stage_third(4)
    stage_z(6)
    stage_z(7)
    stage_z(8)
    out_second()
    stage_half(1)
    stage_third(5)
    stage_half(2)
    stage_third(6)
    stage_third(7)
    stage_half(3)
    stage_third(8)
    stage_half(4)
    stage_half(5)
    stage_half(6)
    out_third()
    for s in range(9):
        stage_end(s)

    before_attention = len(sent)
    arrive(normed.at[1 - core], "normed")
    rows = normed[...].reshape(256, 1024)
    causal = lax.broadcasted_iota(jnp.int32, (128, 128), 0) >= lax.broadcasted_iota(jnp.int32, (128, 128), 1)
    heads = [[], []]
    for h in range(NX):
        qkv = jnp.dot(rows, gq[h].reshape(1024, QKV), preferred_element_type=jnp.float32).astype(jnp.bfloat16)
        for s in range(2):
            piece = qkv[s * 128 : (s + 1) * 128]
            q, k, v = piece[:, 0:128], piece[:, 128:256], piece[:, 256:384]
            scores = lax.dot_general(
                q, k, (((1,), (1,)), ((), ())), preferred_element_type=jnp.float32
            ) / math.sqrt(HEAD_DIM)
            raised = jnp.where(causal, jnp.exp(jnp.where(causal, scores, 0.0)), 0.0)
            probs = (raised / jnp.sum(raised, axis=-1, keepdims=True)).astype(jnp.bfloat16)
            heads[s].append(jnp.dot(probs, v, preferred_element_type=jnp.float32).astype(jnp.bfloat16))
    out_end()
    wide = [jnp.concatenate(heads[i], axis=1) for i in range(2)]
    mine_first = core == 0
    other_heads = jnp.where(mine_first, wide[1], wide[0])
    own_heads = jnp.where(mine_first, wide[0], wide[1])

    def project(rows_in):
        total = jnp.zeros((128, 1024), jnp.float32)
        for h in range(NX):
            total = total + lax.dot_general(
                rows_in[:, h * 128 : (h + 1) * 128],
                go[h].reshape(1024, 128),
                (((1,), (1,)), ((), ())),
                preferred_element_type=jnp.float32,
            )
        return total

    part[...] = project(other_heads).astype(jnp.bfloat16)
    send(part, swap, "swap", sibling)
    stream = tok_ref[...].astype(jnp.float32) + project(own_heads)
    drain(before_attention)
    arrive(swap, "swap")
    stream = stream + swap[...].astype(jnp.float32)
    hidden[...] = stream
    expert_in = rms_scale(stream, gain_e_ref[...]).astype(jnp.bfloat16)
    g[0, y] = expert_in[:, 0:HALF]
    g[1, x] = expert_in[:, HALF : 2 * HALF]

    for color in range(2):
        p, d = lines[color]
        for k in (1, 3):
            send(g.at[color, p], g.at[color, p], ("g", color, k), dev(color, dp=k))

    def first_near(color, k):
        p, d = lines[color]
        arrive(g.at[color, (p - k + 4) % 4], ("g", color, k))
        i = 0 if k == 1 else 1
        block = g.at[color, (p - k + 4) % 4, pl.ds(64 * i, 64)]
        send(block, block, ("g2", color, k), dev(color, dp=k))

    def first_last(color):
        p, d = lines[color]
        for i, k in enumerate((1, 3)):
            arrive(g.at[color, (p + 2) % 4, pl.ds(64 * i, 64)], ("g2", color, k))

    slot_ids = lax.broadcasted_iota(jnp.int32, (SLOTS, 128), 0).astype(jnp.float32)

    def spread(color, k, weighted):
        p, d = lines[color]
        table = ibuf[color, (p + k) % 4]
        blocks = []
        for i in range(8):
            hit = table[i : i + 1] == slot_ids
            blocks.append(jnp.where(hit, table[8 + i : 9 + i] if weighted else 1.0, 0.0))
        return jnp.concatenate(blocks, axis=0)

    def dispatch(color, k):
        p, d = lines[color]
        seq = (p + k) % 4
        rows = jnp.dot(
            spread(color, k, False).astype(jnp.bfloat16), g[color, seq], preferred_element_type=jnp.float32
        ).astype(jnp.bfloat16)
        disp[color, k] = rows.reshape(4, 2, SLOTS, HALF)
        target = r.at[color, d, seq, core]
        for dd in (2, 1, -1):
            for to in range(2):
                src = disp.at[color, k, (d + dd + 4) % 4, to]
                send(src, target, ("d", color, k, dd), dev(color, dd=dd, to=to), width=2)
        send(disp.at[color, k, d, 1 - core], target, ("d", color, k, 0), sibling)
        local(disp.at[color, k, d, core], target, ("d", color, k, "here"))

    def arrivals(kind, color, k, dd, block):
        if dd == 0:
            arrive(block(core), (kind, color, k, "here"))
            arrive(block(1 - core), (kind, color, k, 0))
            return
        for from_core in range(2):
            arrive(block(from_core), (kind, color, k, 2 if dd == 2 else -dd), from_core)

    def group(index, xs, ys):
        places = [(kx, ky) for kx in xs for ky in ys]
        for kx, ky in places:
            column, row = (x + kx) % 4, (y + ky) % 4
            arrivals("d", 0, ky, STEP[kx], lambda c: r.at[0, column, row, c])
            arrivals("d", 1, kx, STEP[ky], lambda c: r.at[1, row, column, c])
        low = [r[0, (x + kx) % 4, (y + ky) % 4].reshape(2 * SLOTS, HALF) for kx, ky in places]
        high = [r[1, (y + ky) % 4, (x + kx) % 4].reshape(2 * SLOTS, HALF) for kx, ky in places]
        low, high = jnp.concatenate(low, axis=0), jnp.concatenate(high, axis=0)

        def product(weight):
            by_row = (((1,), (1,)), ((), ()))
            return lax.dot_general(
                low, weight[:, 0:HALF], by_row, preferred_element_type=jnp.float32
            ) + lax.dot_general(high, weight[:, HALF : 2 * HALF], by_row, preferred_element_type=jnp.float32)

        gate, up = product(wg), product(wu)
        inner = (gate / (1.0 + jnp.exp(-gate)) * up).astype(jnp.bfloat16)
        result = jnp.dot(inner, wd[...], preferred_element_type=jnp.float32).astype(jnp.bfloat16)
        res[0, index] = result[:, 0:HALF].reshape(4, 2, SLOTS, HALF)
        res[1, index] = result[:, HALF : 2 * HALF].reshape(4, 2, SLOTS, HALF)
        for i, (kx, ky) in enumerate(places):
            for color, kk, dd in ((0, ky, STEP[kx]), (1, kx, STEP[ky])):
                p, d = lines[color]
                target = cbuf.at[color, d, core, (p + kk) % 4]
                if dd == 0:
                    send(res.at[color, index, i, 1 - core], target, ("r", color, kk, 0), sibling)
                    local(res.at[color, index, i, core], target, ("r", color, kk, "here"))
                else:
                    for to in range(2):
                        src = res.at[color, index, i, to]
                        send(src, target, ("r", color, kk, dd), dev(color, dd=dd, to=to), width=2)

    def combine(color, k):
        p, d = lines[color]
        seq = (p + k) % 4
        for dd in (0, 1, -1, 2):
            arrivals("r", color, k, dd, lambda c: cbuf.at[color, (d + dd + 4) % 4, c, seq])
        scale = spread(color, k, True)
        high = scale.astype(jnp.bfloat16)
        low = (scale - high.astype(jnp.float32)).astype(jnp.bfloat16)
        rows = cbuf[color, :, :, pl.ds(seq, 1)].reshape(256, HALF)
        total = 0.0
        for term in (high, low):
            total = total + lax.dot_general(
                term, rows, (((0,), (0,)), ((), ())), preferred_element_type=jnp.float32
            )
        if k == 0:
            own_sum[color] = total
            return
        sbuf[color, k] = total.astype(jnp.bfloat16)
        send(sbuf.at[color, k], f.at[color, k], ("f", color, k), dev(color, dp=k))

    both = (0, 1)
    for color in both:
        dispatch(color, 0)
    for color in both:
        for k in (1, 3, 2):
            arrive(ibuf.at[color, (lines[color][0] - k + 4) % 4], ("info", color, k))
    for k in (1, 3):
        for color in both:
            first_near(color, k)
    for k in (1, 3):
        for color in both:
            dispatch(color, (4 - k) % 4)
    for color in both:
        first_last(color)
        dispatch(color, 2)
    before_groups = len(sent)
    arrive(wg, "wg")
    arrive(wu, "wu")
    arrive(wd, "wd")
    group(0, (1, 3), (1, 3))
    group(1, (0, 2), (1, 3))
    group(2, (1, 3), (0, 2))
    group(3, (0, 2), (0, 2))
    drain(before_groups)
    for k in (1, 3):
        combine(0, k)
    for k in (1, 3):
        combine(1, k)
    for k in (2, 0):
        for color in both:
            combine(color, k)
    for color in (1, 0):
        cols = pl.ds(HALF * color, HALF)
        total = hidden[:, cols] + own_sum[color]
        for k in (1, 3, 2):
            arrive(f.at[color, k], ("f", color, k))
            total = total + f[color, k].astype(jnp.float32)
        out_ref[:, cols] = total.astype(out_ref.dtype)
    drain(len(sent))


def per_device(
    tokens,
    attention_gain,
    attention_in,
    attention_out,
    expert_gain,
    routes,
    route_weights,
    gate_weight,
    up_weight,
    down_weight,
):
    rows, model = tokens.shape
    width = gate_weight.shape[2]
    vmem = pl.BlockSpec(memory_space=pltpu.VMEM)
    hbm = pl.BlockSpec(memory_space=pl.ANY)
    blocks = (SLOTS, HALF)
    scratch = [
        (tokens.shape, jnp.bfloat16),
        ((1, model), jnp.float32),
        (attention_in.shape, jnp.bfloat16),
        (attention_out.shape, jnp.bfloat16),
        ((1, model), jnp.float32),
        (routes.shape[::-1], jnp.int32),
        (routes.shape[::-1], jnp.float32),
        ((8, 2, QKV), jnp.bfloat16),
        ((8, 2, HEAD_DIM), jnp.bfloat16),
        ((8, 2, QKV), jnp.bfloat16),
        ((8, 2, HEAD_DIM), jnp.bfloat16),
        ((NX, NZ, NY, 16, QKV), jnp.bfloat16),
        ((NX, NZ, NY, 16, HEAD_DIM), jnp.bfloat16),
        ((2, rows, model), jnp.bfloat16),
        ((rows, model), jnp.bfloat16),
        ((rows, model), jnp.bfloat16),
        ((rows, model), jnp.float32),
        ((width, model), jnp.bfloat16),
        ((width, model), jnp.bfloat16),
        ((width, model), jnp.bfloat16),
        ((2, 4, 16, rows), jnp.float32),
        ((2, 4, 16, rows), jnp.float32),
        ((2, 4, rows, HALF), jnp.bfloat16),
        ((2, 4, 4, 2) + blocks, jnp.bfloat16),
        ((2, 4, 4, 2) + blocks, jnp.bfloat16),
        ((2, 4, 4, 2) + blocks, jnp.bfloat16),
        ((2, 4, 2, 4) + blocks, jnp.bfloat16),
        ((2, 4, rows, HALF), jnp.bfloat16),
        ((2, 4, rows, HALF), jnp.bfloat16),
        ((2, rows, HALF), jnp.float32),
    ]
    mixed = pl.pallas_call(
        layer_kernel,
        out_shape=jax.ShapeDtypeStruct((rows, model), jnp.bfloat16),
        in_specs=[hbm] * 10,
        out_specs=vmem,
        scratch_shapes=[pltpu.VMEM(shape, dtype) for shape, dtype in scratch]
        + [pltpu.SemaphoreType.DMA((SENDS,)), pltpu.SemaphoreType.DMA((RECVS,))],
        compiler_params=pltpu.CompilerParams(collective_id=0, has_side_effects=True),
        name="layer",
    )(
        tokens,
        attention_gain.reshape(1, model),
        attention_in,
        attention_out,
        expert_gain.reshape(1, model),
        routes.T,
        route_weights.T,
        gate_weight[0].T,
        up_weight[0].T,
        down_weight[0],
    )
    return mixed.astype(jnp.bfloat16)


def solution(mesh):
    placed = (
        P(("fsdp", "expert"), None),
        P(),
        P(("fsdp", "expert"), None),
        P(("fsdp", "expert"), None),
        P(),
        P(("fsdp", "expert"), None),
        P(("fsdp", "expert"), None),
        P("expert", None, None),
        P("expert", None, None),
        P("expert", None, None),
    )
    return jax.shard_map(
        per_device,
        mesh=mesh,
        in_specs=placed,
        out_specs=P(("fsdp", "expert"), None),
        check_vma=False,
    )
```

```python
import math

import jax
import jax.numpy as jnp
from jax import lax
from jax.experimental import pallas as pl
from jax.experimental.pallas import tpu as pltpu
from jax.sharding import PartitionSpec as P

MESH = pl.DeviceIdType.MESH
HEAD_DIM = 128
NX, NY, NZ = 4, 4, 16
SLOTS = 32
HALF = 512
QKV = 3 * HEAD_DIM
STEP = {0: 0, 1: 1, 3: -1, 2: 2}
LATE = 7
SENDS, RECVS = 299, 325


def rms_scale(inputs, scale_gain):
    mean_square = jnp.mean(inputs * inputs, axis=-1, keepdims=True)
    return inputs * lax.rsqrt(mean_square + 1e-06) * scale_gain


def place():
    z = lax.axis_index("fsdp")
    e = lax.axis_index("expert")
    return (e // 2) % NX, e // (2 * NX), z, e % 2


def expert_at(x, y, core):
    return (y * NX + x) * 2 + core


def layer_kernel(
    tok_hbm,
    gain_a_hbm,
    ain_hbm,
    aout_hbm,
    gain_e_hbm,
    routes_hbm,
    rw_hbm,
    wg_hbm,
    wu_hbm,
    wd_hbm,
    out_ref,
    tok_ref,
    gain_a_ref,
    ain_ref,
    aout_ref,
    gain_e_ref,
    routes_ref,
    rw_ref,
    cut_q,
    cut_o,
    ex_q,
    ex_o,
    gq,
    go,
    normed,
    part,
    swap,
    hidden,
    wg,
    wu,
    wd,
    info,
    ibuf,
    g,
    disp,
    r,
    res,
    cbuf,
    sbuf,
    f,
    own_sum,
    ss,
    rv,
):
    x, y, z, core = place()
    j = 2 * x + core
    lines = ((y, x), (x, y))

    def dev(color, dp=0, dd=0, to=None):
        p, d = lines[color]
        p, d = (p + dp + 4) % 4, (d + dd + 4) % 4
        to = core if to is None else to
        return {"expert": expert_at(d, p, to) if color == 0 else expert_at(p, d, to)}

    def up_z(dz):
        return {"fsdp": (z + dz + NZ) % NZ}

    def peer(d):
        return {"expert": y * 2 * NX + (j + d) % 8}

    sibling = {"expert": expert_at(x, y, 1 - core)}
    near = [s * d for d in (4, 1, 2, 3) for s in (1, -1)]
    barrier = pltpu.get_barrier_semaphore()
    partners = [up_z(d) for d in near]
    partners += [dev(0, dp=d, to=to) for d in (2, 1, -1) for to in (0, 1)]
    partners += [peer(d) for d in range(1, 8)]
    for ident in partners:
        pl.semaphore_signal(barrier, inc=1, device_id=ident, device_id_type=MESH)

    sent, bases = [], {}

    def base(name, width=1):
        if name not in bases:
            bases[name] = sum(w for _, w in bases.values()), width
        return bases[name][0]

    def send(src, dst, name, ident, width=1):
        at = base(name, width)
        copy = pltpu.make_async_remote_copy(
            src_ref=src,
            dst_ref=dst,
            send_sem=ss.at[len(sent)],
            recv_sem=rv.at[at + core if width == 2 else at],
            device_id=ident,
            device_id_type=MESH,
        )
        copy.start()
        sent.append(copy.wait_send)

    drained = [0]

    def drain(upto):
        for wait in sent[drained[0] : upto]:
            wait()
        drained[0] = upto

    def local(src, dst, name):
        pltpu.make_async_copy(src, dst, rv.at[base(name)]).start()

    def arrive(dst, name, which=0):
        pltpu.make_async_copy(dst, dst, rv.at[base(name) + which]).wait()

    staged = (
        (ain_hbm, ain_ref, "ain"),
        (aout_hbm, aout_ref, "aout"),
        (tok_hbm, tok_ref, "tok"),
        (gain_a_hbm, gain_a_ref, "gain_a"),
        (routes_hbm, routes_ref, "routes"),
        (rw_hbm, rw_ref, "rw"),
        (gain_e_hbm, gain_e_ref, "gain_e"),
    )
    for source, place_in, name in staged:
        local(source, place_in, name)
    for _, place_in, name in staged[:2]:
        arrive(place_in, name)
    for h in range(8):
        for i in range(3):
            cut_q[h, :, i * 128 : (i + 1) * 128] = ain_ref[:, (8 * i + h) * 128 : (8 * i + h + 1) * 128]
        cut_o[h] = aout_ref[:, h * 128 : (h + 1) * 128]
    ex_q[j] = cut_q[j]
    ex_o[j] = cut_o[j]
    pl.semaphore_wait(barrier, len(partners))

    for d in (4, 3, 5, 2, 6, 1, 7):
        send(cut_q.at[(j + d) % 8], ex_q.at[j], ("ex_q", d), peer(d))
    for d in (4, 3, 5, 2, 6, 1, 7):
        send(cut_o.at[(j + d) % 8], ex_o.at[j], ("ex_o", d), peer(d))
    for _, place_in, name in staged[2:]:
        arrive(place_in, name)
    normed[core] = rms_scale(tok_ref[...].astype(jnp.float32), gain_a_ref[...]).astype(jnp.bfloat16)
    send(normed.at[core], normed.at[core], "normed", sibling)
    for source, place_in, name in ((wg_hbm, wg, "wg"), (wu_hbm, wu, "wu"), (wd_hbm, wd, "wd")):
        local(source, place_in, name)

    expert_ids = lax.broadcasted_iota(jnp.int32, (32, 128), 0)
    chosen = jnp.zeros((32, 128), jnp.float32)
    weight_of = jnp.zeros((32, 128), jnp.float32)
    for k in range(routes_ref.shape[0]):
        hit = routes_ref[k : k + 1, :] == expert_ids
        chosen = jnp.where(hit, 1.0, chosen)
        weight_of = jnp.where(hit, rw_ref[k : k + 1, :], weight_of)
    earlier = lax.broadcasted_iota(jnp.int32, (128, 128), 0) < lax.broadcasted_iota(jnp.int32, (128, 128), 1)
    slot_of = jnp.dot(
        chosen.astype(jnp.bfloat16),
        jnp.where(earlier, 1.0, 0.0).astype(jnp.bfloat16),
        preferred_element_type=jnp.float32,
    )
    slot_of = jnp.where(chosen > 0.0, slot_of, -1.0)
    for at, table in ((0, slot_of), (8, weight_of)):
        for i in range(4):
            info[0, i, at : at + 8] = table[8 * i : 8 * i + 8]
            for q in range(4):
                info[1, i, at + 2 * q : at + 2 * q + 2] = table[8 * q + 2 * i : 8 * q + 2 * i + 2]

    def join(ref):
        pieces = [ref[i].astype(jnp.float32) for i in range(8)]
        return jnp.concatenate(pieces, axis=0).astype(jnp.bfloat16)

    for d in (4, 3, 5, 2, 6, 1, 7):
        arrive(ex_q.at[(j + d) % 8], ("ex_q", d))
    gq[x, z, y] = join(ex_q)
    mine = gq.at[x, z, y]

    def second(color, s, zs):
        here = gq.at[x, zs, y]
        for dp in (2, 1, -1):
            send(here, here, ("p2", color, s, dp), dev(color, dp=dp))

    for d in near:
        color = 0 if d > 0 else 1
        send(mine, mine, ("z", color, abs(d)), up_z(d))
        if d == -4:
            second(0, 0, z)

    for d in (4, 3, 5, 2, 6, 1, 7):
        arrive(ex_o.at[(j + d) % 8], ("ex_o", d))
    go[x, z, y] = join(ex_o)
    for d in near:
        send(go.at[x, z, y], go.at[x, z, y], ("zo", 0 if d > 0 else 1, abs(d)), up_z(d))
    for color in range(2):
        p, d = lines[color]
        for k in (1, 3, 2):
            send(info.at[color, (p + k) % 4], ibuf.at[color, p], ("info", color, k), dev(color, dp=k))
        ibuf[color, p] = info[color, p]

    def chunks(s):
        found = []
        if s <= NZ // 2 - 1:
            found.append((0, (z - s + NZ) % NZ))
        if s >= 1:
            found.append((1, (z + s) % NZ))
        return found

    def passed_on(ref, kind, color, zs):
        here = ref.at[x, zs, y]
        for i in range(3 + color, 0, -1):
            send(here, here, (kind, color, 4 + i), up_z(i if color == 0 else -i))

    def stage_z(s):
        for color, zs in chunks(s):
            arrive(gq.at[x, zs, y], ("z", color, s))
            if s == 4:
                passed_on(gq, "z", color, zs)
            second(color, s, zs)

    def row_of(color, zs, index):
        return gq.at[x, zs, index] if color == 0 else gq.at[index, zs, y]

    def block_of(color, zs, index):
        return gq.at[index, zs] if color == 0 else gq.at[:, zs, index]

    def half_of(color, zs, index, i):
        part = pl.ds(2 * i, 2)
        return gq.at[index, zs, part] if color == 0 else gq.at[part, zs, index]

    def stage_third(s):
        for color, zs in chunks(s):
            p, d = lines[color]
            for dp in (1, -1, 2):
                arrive(row_of(color, zs, (p - dp + 4) % 4), ("p2", color, s, dp))
            for dd in (1, -1) if s < LATE else (2, 1, -1):
                send(block_of(color, zs, d), block_of(color, zs, d), ("p3", color, s, dd), dev(color, dd=dd))

    def stage_half(s):
        for color, zs in chunks(s):
            p, d = lines[color]
            for dd in (1, -1):
                arrive(block_of(color, zs, (d - dd + 4) % 4), ("p3", color, s, dd))
            for i, dd in enumerate((1, -1)):
                half = half_of(color, zs, (d - dd + 4) % 4, i)
                send(half, half, ("p4", color, s, i), dev(color, dd=dd))

    def stage_end(s):
        for color, zs in chunks(s):
            p, d = lines[color]
            if s >= LATE:
                for dd in (1, -1, 2):
                    arrive(block_of(color, zs, (d - dd + 4) % 4), ("p3", color, s, dd))
                continue
            for i in range(2):
                arrive(half_of(color, zs, (d + 2) % 4, i), ("p4", color, s, i))

    def out_pass_on():
        for color in range(2):
            zs = (z - 4 + NZ) % NZ if color == 0 else (z + 4) % NZ
            arrive(go.at[x, zs, y], ("zo", color, 4))
            passed_on(go, "zo", color, zs)

    def out_row(color, index):
        zs = pl.ds(8 * color, 8)
        return go.at[x, zs, index] if color == 0 else go.at[index, zs, y]

    def out_block(color, index):
        zs = pl.ds(8 * color, 8)
        return go.at[index, zs] if color == 0 else go.at[:, zs, index]

    def out_second():
        for s in range(1, 9):
            for color, zs in chunks(s):
                if s != 4:
                    arrive(go.at[x, zs, y], ("zo", color, s))
        for color in range(2):
            p, d = lines[color]
            for dp in (2, 1, -1):
                send(out_row(color, p), out_row(color, p), ("o2", color, dp), dev(color, dp=dp))

    def out_third():
        for color in range(2):
            p, d = lines[color]
            for dp in (1, -1, 2):
                arrive(out_row(color, (p - dp + 4) % 4), ("o2", color, dp))
            for dd in (2, 1, -1):
                send(out_block(color, d), out_block(color, d), ("o3", color, dd), dev(color, dd=dd))

    def out_end():
        for color in range(2):
            p, d = lines[color]
            for dd in (1, -1, 2):
                arrive(out_block(color, (d - dd + 4) % 4), ("o3", color, dd))

    stage_z(1)
    stage_z(2)
    stage_z(3)
    stage_z(4)
    stage_third(0)
    out_pass_on()
    stage_third(1)
    stage_third(2)
    stage_z(5)
    stage_third(3)
    stage_half(0)
    stage_third(4)
    stage_z(6)
    stage_z(7)
    stage_z(8)
    out_second()
    stage_half(1)
    stage_third(5)
    stage_half(2)
    stage_third(6)
    stage_third(7)
    stage_half(3)
    stage_third(8)
    stage_half(4)
    stage_half(5)
    stage_half(6)
    out_third()
    for s in range(9):
        stage_end(s)

    before_attention = len(sent)
    arrive(normed.at[1 - core], "normed")
    rows = normed[...].reshape(256, 1024)
    causal = lax.broadcasted_iota(jnp.int32, (128, 128), 0) >= lax.broadcasted_iota(jnp.int32, (128, 128), 1)
    heads = [[], []]
    for h in range(NX):
        qkv = jnp.dot(rows, gq[h].reshape(1024, QKV), preferred_element_type=jnp.float32).astype(jnp.bfloat16)
        for s in range(2):
            piece = qkv[s * 128 : (s + 1) * 128]
            q, k, v = piece[:, 0:128], piece[:, 128:256], piece[:, 256:384]
            scores = lax.dot_general(
                q, k, (((1,), (1,)), ((), ())), preferred_element_type=jnp.float32
            ) / math.sqrt(HEAD_DIM)
            raised = jnp.where(causal, jnp.exp(jnp.where(causal, scores, 0.0)), 0.0)
            probs = (raised / jnp.sum(raised, axis=-1, keepdims=True)).astype(jnp.bfloat16)
            heads[s].append(jnp.dot(probs, v, preferred_element_type=jnp.float32).astype(jnp.bfloat16))
    out_end()
    wide = [jnp.concatenate(heads[i], axis=1) for i in range(2)]
    mine_first = core == 0
    other_heads = jnp.where(mine_first, wide[1], wide[0])
    own_heads = jnp.where(mine_first, wide[0], wide[1])

    def project(rows_in):
        total = jnp.zeros((128, 1024), jnp.float32)
        for h in range(NX):
            total = total + lax.dot_general(
                rows_in[:, h * 128 : (h + 1) * 128],
                go[h].reshape(1024, 128),
                (((1,), (1,)), ((), ())),
                preferred_element_type=jnp.float32,
            )
        return total

    part[...] = project(other_heads).astype(jnp.bfloat16)
    send(part, swap, "swap", sibling)
    stream = tok_ref[...].astype(jnp.float32) + project(own_heads)
    drain(before_attention)
    arrive(swap, "swap")
    stream = stream + swap[...].astype(jnp.float32)
    hidden[...] = stream
    expert_in = rms_scale(stream, gain_e_ref[...]).astype(jnp.bfloat16)
    g[0, y] = expert_in[:, 0:HALF]
    g[1, x] = expert_in[:, HALF : 2 * HALF]

    for color in range(2):
        p, d = lines[color]
        for k in (1, 3):
            send(g.at[color, p], g.at[color, p], ("g", color, k), dev(color, dp=k))

    def first_near(color, k):
        p, d = lines[color]
        arrive(g.at[color, (p - k + 4) % 4], ("g", color, k))
        i = 0 if k == 1 else 1
        block = g.at[color, (p - k + 4) % 4, pl.ds(64 * i, 64)]
        send(block, block, ("g2", color, k), dev(color, dp=k))

    def first_last(color):
        p, d = lines[color]
        for i, k in enumerate((1, 3)):
            arrive(g.at[color, (p + 2) % 4, pl.ds(64 * i, 64)], ("g2", color, k))

    slot_ids = lax.broadcasted_iota(jnp.int32, (SLOTS, 128), 0).astype(jnp.float32)

    def spread(color, k, weighted):
        p, d = lines[color]
        table = ibuf[color, (p + k) % 4]
        blocks = []
        for i in range(8):
            hit = table[i : i + 1] == slot_ids
            blocks.append(jnp.where(hit, table[8 + i : 9 + i] if weighted else 1.0, 0.0))
        return jnp.concatenate(blocks, axis=0)

    def dispatch(color, k):
        p, d = lines[color]
        seq = (p + k) % 4
        rows = jnp.dot(
            spread(color, k, False).astype(jnp.bfloat16), g[color, seq], preferred_element_type=jnp.float32
        ).astype(jnp.bfloat16)
        disp[color, k] = rows.reshape(4, 2, SLOTS, HALF)
        target = r.at[color, d, seq, core]
        for dd in (2, 1, -1):
            for to in range(2):
                src = disp.at[color, k, (d + dd + 4) % 4, to]
                send(src, target, ("d", color, k, dd), dev(color, dd=dd, to=to), width=2)
        send(disp.at[color, k, d, 1 - core], target, ("d", color, k, 0), sibling)
        local(disp.at[color, k, d, core], target, ("d", color, k, "here"))

    def arrivals(kind, color, k, dd, block):
        if dd == 0:
            arrive(block(core), (kind, color, k, "here"))
            arrive(block(1 - core), (kind, color, k, 0))
            return
        for from_core in range(2):
            arrive(block(from_core), (kind, color, k, 2 if dd == 2 else -dd), from_core)

    def group(index, xs, ys):
        places = [(kx, ky) for kx in xs for ky in ys]
        for kx, ky in places:
            column, row = (x + kx) % 4, (y + ky) % 4
            arrivals("d", 0, ky, STEP[kx], lambda c: r.at[0, column, row, c])
            arrivals("d", 1, kx, STEP[ky], lambda c: r.at[1, row, column, c])
        low = [r[0, (x + kx) % 4, (y + ky) % 4].reshape(2 * SLOTS, HALF) for kx, ky in places]
        high = [r[1, (y + ky) % 4, (x + kx) % 4].reshape(2 * SLOTS, HALF) for kx, ky in places]
        low, high = jnp.concatenate(low, axis=0), jnp.concatenate(high, axis=0)

        def product(weight):
            by_row = (((1,), (1,)), ((), ()))
            return lax.dot_general(
                low, weight[:, 0:HALF], by_row, preferred_element_type=jnp.float32
            ) + lax.dot_general(high, weight[:, HALF : 2 * HALF], by_row, preferred_element_type=jnp.float32)

        gate, up = product(wg), product(wu)
        inner = (gate / (1.0 + jnp.exp(-gate)) * up).astype(jnp.bfloat16)
        result = jnp.dot(inner, wd[...], preferred_element_type=jnp.float32).astype(jnp.bfloat16)
        res[0, index] = result[:, 0:HALF].reshape(4, 2, SLOTS, HALF)
        res[1, index] = result[:, HALF : 2 * HALF].reshape(4, 2, SLOTS, HALF)
        for i, (kx, ky) in enumerate(places):
            for color, kk, dd in ((0, ky, STEP[kx]), (1, kx, STEP[ky])):
                p, d = lines[color]
                target = cbuf.at[color, d, core, (p + kk) % 4]
                if dd == 0:
                    send(res.at[color, index, i, 1 - core], target, ("r", color, kk, 0), sibling)
                    local(res.at[color, index, i, core], target, ("r", color, kk, "here"))
                else:
                    for to in range(2):
                        src = res.at[color, index, i, to]
                        send(src, target, ("r", color, kk, dd), dev(color, dd=dd, to=to), width=2)

    def scales(color, k):
        scale = spread(color, k, True)
        high = scale.astype(jnp.bfloat16)
        return high, (scale - high.astype(jnp.float32)).astype(jnp.bfloat16)

    def combine(color, k, terms):
        p, d = lines[color]
        seq = (p + k) % 4
        for dd in (0, 1, -1, 2):
            arrivals("r", color, k, dd, lambda c: cbuf.at[color, (d + dd + 4) % 4, c, seq])
        rows = cbuf[color, :, :, pl.ds(seq, 1)].reshape(256, HALF)
        total = 0.0
        for term in terms:
            total = total + lax.dot_general(
                term, rows, (((0,), (0,)), ((), ())), preferred_element_type=jnp.float32
            )
        if k == 0:
            own_sum[color] = total
            return
        sbuf[color, k] = total.astype(jnp.bfloat16)
        send(sbuf.at[color, k], f.at[color, k], ("f", color, k), dev(color, dp=k))

    both = (0, 1)
    for color in both:
        dispatch(color, 0)
    for color in both:
        for k in (1, 3, 2):
            arrive(ibuf.at[color, (lines[color][0] - k + 4) % 4], ("info", color, k))
    for k in (1, 3):
        for color in both:
            first_near(color, k)
    for k in (1, 3):
        for color in both:
            dispatch(color, (4 - k) % 4)
    for color in both:
        first_last(color)
        dispatch(color, 2)
    before_groups = len(sent)
    arrive(wg, "wg")
    arrive(wu, "wu")
    arrive(wd, "wd")
    group(0, (1, 3), (1, 3))
    group(1, (0, 2), (1, 3))
    group(2, (1, 3), (0, 2))
    group(3, (0, 2), (0, 2))
    drain(before_groups)
    for color in both:
        for k in (1, 3):
            combine(color, k, scales(color, k))
    ready = {(color, k): scales(color, k) for k in (2, 0) for color in both}
    for k in (2, 0):
        for color in both:
            combine(color, k, ready[color, k])
    for color in (1, 0):
        cols = pl.ds(HALF * color, HALF)
        total = hidden[:, cols] + own_sum[color]
        for k in (1, 3, 2):
            arrive(f.at[color, k], ("f", color, k))
            total = total + f[color, k].astype(jnp.float32)
        out_ref[:, cols] = total.astype(out_ref.dtype)
    drain(len(sent))


def per_device(
    tokens,
    attention_gain,
    attention_in,
    attention_out,
    expert_gain,
    routes,
    route_weights,
    gate_weight,
    up_weight,
    down_weight,
):
    rows, model = tokens.shape
    width = gate_weight.shape[2]
    vmem = pl.BlockSpec(memory_space=pltpu.VMEM)
    hbm = pl.BlockSpec(memory_space=pl.ANY)
    blocks = (SLOTS, HALF)
    scratch = [
        (tokens.shape, jnp.bfloat16),
        ((1, model), jnp.float32),
        (attention_in.shape, jnp.bfloat16),
        (attention_out.shape, jnp.bfloat16),
        ((1, model), jnp.float32),
        (routes.shape[::-1], jnp.int32),
        (routes.shape[::-1], jnp.float32),
        ((8, 2, QKV), jnp.bfloat16),
        ((8, 2, HEAD_DIM), jnp.bfloat16),
        ((8, 2, QKV), jnp.bfloat16),
        ((8, 2, HEAD_DIM), jnp.bfloat16),
        ((NX, NZ, NY, 16, QKV), jnp.bfloat16),
        ((NX, NZ, NY, 16, HEAD_DIM), jnp.bfloat16),
        ((2, rows, model), jnp.bfloat16),
        ((rows, model), jnp.bfloat16),
        ((rows, model), jnp.bfloat16),
        ((rows, model), jnp.float32),
        ((width, model), jnp.bfloat16),
        ((width, model), jnp.bfloat16),
        ((width, model), jnp.bfloat16),
        ((2, 4, 16, rows), jnp.float32),
        ((2, 4, 16, rows), jnp.float32),
        ((2, 4, rows, HALF), jnp.bfloat16),
        ((2, 4, 4, 2) + blocks, jnp.bfloat16),
        ((2, 4, 4, 2) + blocks, jnp.bfloat16),
        ((2, 4, 4, 2) + blocks, jnp.bfloat16),
        ((2, 4, 2, 4) + blocks, jnp.bfloat16),
        ((2, 4, rows, HALF), jnp.bfloat16),
        ((2, 4, rows, HALF), jnp.bfloat16),
        ((2, rows, HALF), jnp.float32),
    ]
    mixed = pl.pallas_call(
        layer_kernel,
        out_shape=jax.ShapeDtypeStruct((rows, model), jnp.bfloat16),
        in_specs=[hbm] * 10,
        out_specs=vmem,
        scratch_shapes=[pltpu.VMEM(shape, dtype) for shape, dtype in scratch]
        + [pltpu.SemaphoreType.DMA((SENDS,)), pltpu.SemaphoreType.DMA((RECVS,))],
        compiler_params=pltpu.CompilerParams(collective_id=0, has_side_effects=True),
        name="layer",
    )(
        tokens,
        attention_gain.reshape(1, model),
        attention_in,
        attention_out,
        expert_gain.reshape(1, model),
        routes.T,
        route_weights.T,
        gate_weight[0].T,
        up_weight[0].T,
        down_weight[0],
    )
    return mixed.astype(jnp.bfloat16)


def solution(mesh):
    placed = (
        P(("fsdp", "expert"), None),
        P(),
        P(("fsdp", "expert"), None),
        P(("fsdp", "expert"), None),
        P(),
        P(("fsdp", "expert"), None),
        P(("fsdp", "expert"), None),
        P("expert", None, None),
        P("expert", None, None),
        P("expert", None, None),
    )
    return jax.shard_map(
        per_device,
        mesh=mesh,
        in_specs=placed,
        out_specs=P(("fsdp", "expert"), None),
        check_vma=False,
    )
```

```python
import math

import jax
import jax.numpy as jnp
from jax import lax
from jax.experimental import pallas as pl
from jax.experimental.pallas import tpu as pltpu
from jax.sharding import PartitionSpec as P

MESH = pl.DeviceIdType.MESH
HEAD_DIM = 128
NX, NY, NZ = 4, 4, 16
SLOTS = 32
HALF = 512
QKV = 3 * HEAD_DIM
STEP = {0: 0, 1: 1, 3: -1, 2: 2}
LATE = 5
SENDS, RECVS = 295, 321


def rms_scale(inputs, scale_gain):
    mean_square = jnp.mean(inputs * inputs, axis=-1, keepdims=True)
    return inputs * lax.rsqrt(mean_square + 1e-06) * scale_gain


def place():
    z = lax.axis_index("fsdp")
    e = lax.axis_index("expert")
    return (e // 2) % NX, e // (2 * NX), z, e % 2


def expert_at(x, y, core):
    return (y * NX + x) * 2 + core


def layer_kernel(
    tok_hbm,
    gain_a_hbm,
    ain_hbm,
    aout_hbm,
    gain_e_hbm,
    routes_hbm,
    rw_hbm,
    wg_hbm,
    wu_hbm,
    wd_hbm,
    out_ref,
    tok_ref,
    gain_a_ref,
    ain_ref,
    aout_ref,
    gain_e_ref,
    routes_ref,
    rw_ref,
    cut_q,
    cut_o,
    ex_q,
    ex_o,
    gq,
    go,
    normed,
    part,
    swap,
    hidden,
    wg,
    wu,
    wd,
    info,
    ibuf,
    g,
    disp,
    r,
    res,
    cbuf,
    sbuf,
    f,
    own_sum,
    ss,
    rv,
):
    x, y, z, core = place()
    j = 2 * x + core
    lines = ((y, x), (x, y))

    def dev(color, dp=0, dd=0, to=None):
        p, d = lines[color]
        p, d = (p + dp + 4) % 4, (d + dd + 4) % 4
        to = core if to is None else to
        return {"expert": expert_at(d, p, to) if color == 0 else expert_at(p, d, to)}

    def up_z(dz):
        return {"fsdp": (z + dz + NZ) % NZ}

    def peer(d):
        return {"expert": y * 2 * NX + (j + d) % 8}

    sibling = {"expert": expert_at(x, y, 1 - core)}
    near = [s * d for d in (4, 1, 2, 3) for s in (1, -1)]
    barrier = pltpu.get_barrier_semaphore()
    partners = [up_z(d) for d in near]
    partners += [dev(0, dp=d, to=to) for d in (2, 1, -1) for to in (0, 1)]
    partners += [peer(d) for d in range(1, 8)]
    for ident in partners:
        pl.semaphore_signal(barrier, inc=1, device_id=ident, device_id_type=MESH)

    sent, bases = [], {}

    def base(name, width=1):
        if name not in bases:
            bases[name] = sum(w for _, w in bases.values()), width
        return bases[name][0]

    def send(src, dst, name, ident, width=1):
        at = base(name, width)
        copy = pltpu.make_async_remote_copy(
            src_ref=src,
            dst_ref=dst,
            send_sem=ss.at[len(sent)],
            recv_sem=rv.at[at + core if width == 2 else at],
            device_id=ident,
            device_id_type=MESH,
        )
        copy.start()
        sent.append(copy.wait_send)

    drained = [0]

    def drain(upto):
        for wait in sent[drained[0] : upto]:
            wait()
        drained[0] = upto

    def local(src, dst, name):
        pltpu.make_async_copy(src, dst, rv.at[base(name)]).start()

    def arrive(dst, name, which=0):
        pltpu.make_async_copy(dst, dst, rv.at[base(name) + which]).wait()

    staged = (
        (ain_hbm, ain_ref, "ain"),
        (aout_hbm, aout_ref, "aout"),
        (tok_hbm, tok_ref, "tok"),
        (gain_a_hbm, gain_a_ref, "gain_a"),
        (routes_hbm, routes_ref, "routes"),
        (rw_hbm, rw_ref, "rw"),
        (gain_e_hbm, gain_e_ref, "gain_e"),
    )
    for source, place_in, name in staged:
        local(source, place_in, name)
    for _, place_in, name in staged[:2]:
        arrive(place_in, name)
    for h in range(8):
        for i in range(3):
            cut_q[h, :, i * 128 : (i + 1) * 128] = ain_ref[:, (8 * i + h) * 128 : (8 * i + h + 1) * 128]
        cut_o[h] = aout_ref[:, h * 128 : (h + 1) * 128]
    ex_q[j] = cut_q[j]
    ex_o[j] = cut_o[j]
    pl.semaphore_wait(barrier, len(partners))

    for d in (4, 3, 5, 2, 6, 1, 7):
        send(cut_q.at[(j + d) % 8], ex_q.at[j], ("ex_q", d), peer(d))
    for d in (4, 3, 5, 2, 6, 1, 7):
        send(cut_o.at[(j + d) % 8], ex_o.at[j], ("ex_o", d), peer(d))
    for _, place_in, name in staged[2:]:
        arrive(place_in, name)
    normed[core] = rms_scale(tok_ref[...].astype(jnp.float32), gain_a_ref[...]).astype(jnp.bfloat16)
    send(normed.at[core], normed.at[core], "normed", sibling)
    for source, place_in, name in ((wg_hbm, wg, "wg"), (wu_hbm, wu, "wu"), (wd_hbm, wd, "wd")):
        local(source, place_in, name)

    expert_ids = lax.broadcasted_iota(jnp.int32, (32, 128), 0)
    chosen = jnp.zeros((32, 128), jnp.float32)
    weight_of = jnp.zeros((32, 128), jnp.float32)
    for k in range(routes_ref.shape[0]):
        hit = routes_ref[k : k + 1, :] == expert_ids
        chosen = jnp.where(hit, 1.0, chosen)
        weight_of = jnp.where(hit, rw_ref[k : k + 1, :], weight_of)
    earlier = lax.broadcasted_iota(jnp.int32, (128, 128), 0) < lax.broadcasted_iota(jnp.int32, (128, 128), 1)
    slot_of = jnp.dot(
        chosen.astype(jnp.bfloat16),
        jnp.where(earlier, 1.0, 0.0).astype(jnp.bfloat16),
        preferred_element_type=jnp.float32,
    )
    slot_of = jnp.where(chosen > 0.0, slot_of, -1.0)
    for at, table in ((0, slot_of), (8, weight_of)):
        for i in range(4):
            info[0, i, at : at + 8] = table[8 * i : 8 * i + 8]
            for q in range(4):
                info[1, i, at + 2 * q : at + 2 * q + 2] = table[8 * q + 2 * i : 8 * q + 2 * i + 2]

    def join(ref):
        pieces = [ref[i].astype(jnp.float32) for i in range(8)]
        return jnp.concatenate(pieces, axis=0).astype(jnp.bfloat16)

    for d in (4, 3, 5, 2, 6, 1, 7):
        arrive(ex_q.at[(j + d) % 8], ("ex_q", d))
    gq[x, z, y] = join(ex_q)
    mine = gq.at[x, z, y]

    def second(color, s, zs):
        here = gq.at[x, zs, y]
        for dp in (2, 1, -1):
            send(here, here, ("p2", color, s, dp), dev(color, dp=dp))

    for d in near:
        color = 0 if d > 0 else 1
        send(mine, mine, ("z", color, abs(d)), up_z(d))
        if d == -4:
            second(0, 0, z)

    for d in (4, 3, 5, 2, 6, 1, 7):
        arrive(ex_o.at[(j + d) % 8], ("ex_o", d))
    go[x, z, y] = join(ex_o)
    for d in near:
        send(go.at[x, z, y], go.at[x, z, y], ("zo", 0 if d > 0 else 1, abs(d)), up_z(d))
    for color in range(2):
        p, d = lines[color]
        for k in (1, 3, 2):
            send(info.at[color, (p + k) % 4], ibuf.at[color, p], ("info", color, k), dev(color, dp=k))
        ibuf[color, p] = info[color, p]

    def chunks(s):
        found = []
        if s <= NZ // 2 - 1:
            found.append((0, (z - s + NZ) % NZ))
        if s >= 1:
            found.append((1, (z + s) % NZ))
        return found

    def passed_on(ref, kind, color, zs):
        here = ref.at[x, zs, y]
        for i in range(3 + color, 0, -1):
            send(here, here, (kind, color, 4 + i), up_z(i if color == 0 else -i))

    def stage_z(s):
        for color, zs in chunks(s):
            arrive(gq.at[x, zs, y], ("z", color, s))
            if s == 4:
                passed_on(gq, "z", color, zs)
            second(color, s, zs)

    def row_of(color, zs, index):
        return gq.at[x, zs, index] if color == 0 else gq.at[index, zs, y]

    def block_of(color, zs, index):
        return gq.at[index, zs] if color == 0 else gq.at[:, zs, index]

    def half_of(color, zs, index, i):
        part = pl.ds(2 * i, 2)
        return gq.at[index, zs, part] if color == 0 else gq.at[part, zs, index]

    def stage_third(s):
        for color, zs in chunks(s):
            p, d = lines[color]
            for dp in (1, -1, 2):
                arrive(row_of(color, zs, (p - dp + 4) % 4), ("p2", color, s, dp))
            for dd in (1, -1) if s < LATE else (2, 1, -1):
                send(block_of(color, zs, d), block_of(color, zs, d), ("p3", color, s, dd), dev(color, dd=dd))

    def stage_half(s):
        for color, zs in chunks(s):
            p, d = lines[color]
            for dd in (1, -1):
                arrive(block_of(color, zs, (d - dd + 4) % 4), ("p3", color, s, dd))
            for i, dd in enumerate((1, -1)):
                half = half_of(color, zs, (d - dd + 4) % 4, i)
                send(half, half, ("p4", color, s, i), dev(color, dd=dd))

    def stage_end(s):
        for color, zs in chunks(s):
            p, d = lines[color]
            if s >= LATE:
                for dd in (1, -1, 2):
                    arrive(block_of(color, zs, (d - dd + 4) % 4), ("p3", color, s, dd))
                continue
            for i in range(2):
                arrive(half_of(color, zs, (d + 2) % 4, i), ("p4", color, s, i))

    def out_pass_on():
        for color in range(2):
            zs = (z - 4 + NZ) % NZ if color == 0 else (z + 4) % NZ
            arrive(go.at[x, zs, y], ("zo", color, 4))
            passed_on(go, "zo", color, zs)

    def out_row(color, index):
        zs = pl.ds(8 * color, 8)
        return go.at[x, zs, index] if color == 0 else go.at[index, zs, y]

    def out_block(color, index):
        zs = pl.ds(8 * color, 8)
        return go.at[index, zs] if color == 0 else go.at[:, zs, index]

    def out_second():
        for s in range(1, 9):
            for color, zs in chunks(s):
                if s != 4:
                    arrive(go.at[x, zs, y], ("zo", color, s))
        for color in range(2):
            p, d = lines[color]
            for dp in (2, 1, -1):
                send(out_row(color, p), out_row(color, p), ("o2", color, dp), dev(color, dp=dp))

    def out_third():
        for color in range(2):
            p, d = lines[color]
            for dp in (1, -1, 2):
                arrive(out_row(color, (p - dp + 4) % 4), ("o2", color, dp))
            for dd in (2, 1, -1):
                send(out_block(color, d), out_block(color, d), ("o3", color, dd), dev(color, dd=dd))

    def out_end():
        for color in range(2):
            p, d = lines[color]
            for dd in (1, -1, 2):
                arrive(out_block(color, (d - dd + 4) % 4), ("o3", color, dd))

    stage_z(1)
    stage_z(2)
    stage_z(3)
    stage_z(4)
    stage_third(0)
    out_pass_on()
    stage_third(1)
    stage_third(2)
    stage_z(5)
    stage_third(3)
    stage_half(0)
    stage_third(4)
    stage_z(6)
    stage_z(7)
    stage_z(8)
    out_second()
    stage_half(1)
    stage_third(5)
    stage_half(2)
    stage_third(6)
    stage_third(7)
    stage_half(3)
    stage_third(8)
    stage_half(4)
    out_third()
    for s in range(9):
        stage_end(s)

    before_attention = len(sent)
    arrive(normed.at[1 - core], "normed")
    rows = normed[...].reshape(256, 1024)
    causal = lax.broadcasted_iota(jnp.int32, (128, 128), 0) >= lax.broadcasted_iota(jnp.int32, (128, 128), 1)
    heads = [[], []]
    for h in range(NX):
        qkv = jnp.dot(rows, gq[h].reshape(1024, QKV), preferred_element_type=jnp.float32).astype(jnp.bfloat16)
        for s in range(2):
            piece = qkv[s * 128 : (s + 1) * 128]
            q, k, v = piece[:, 0:128], piece[:, 128:256], piece[:, 256:384]
            scores = lax.dot_general(
                q, k, (((1,), (1,)), ((), ())), preferred_element_type=jnp.float32
            ) / math.sqrt(HEAD_DIM)
            raised = jnp.where(causal, jnp.exp(jnp.where(causal, scores, 0.0)), 0.0)
            probs = (raised / jnp.sum(raised, axis=-1, keepdims=True)).astype(jnp.bfloat16)
            heads[s].append(jnp.dot(probs, v, preferred_element_type=jnp.float32).astype(jnp.bfloat16))
    out_end()
    wide = [jnp.concatenate(heads[i], axis=1) for i in range(2)]
    mine_first = core == 0
    other_heads = jnp.where(mine_first, wide[1], wide[0])
    own_heads = jnp.where(mine_first, wide[0], wide[1])

    def project(rows_in):
        total = jnp.zeros((128, 1024), jnp.float32)
        for h in range(NX):
            total = total + lax.dot_general(
                rows_in[:, h * 128 : (h + 1) * 128],
                go[h].reshape(1024, 128),
                (((1,), (1,)), ((), ())),
                preferred_element_type=jnp.float32,
            )
        return total

    part[...] = project(other_heads).astype(jnp.bfloat16)
    send(part, swap, "swap", sibling)
    stream = tok_ref[...].astype(jnp.float32) + project(own_heads)
    drain(before_attention)
    arrive(swap, "swap")
    stream = stream + swap[...].astype(jnp.float32)
    hidden[...] = stream
    expert_in = rms_scale(stream, gain_e_ref[...]).astype(jnp.bfloat16)
    g[0, y] = expert_in[:, 0:HALF]
    g[1, x] = expert_in[:, HALF : 2 * HALF]

    for color in range(2):
        p, d = lines[color]
        for k in (1, 3):
            send(g.at[color, p], g.at[color, p], ("g", color, k), dev(color, dp=k))

    def first_near(color, k):
        p, d = lines[color]
        arrive(g.at[color, (p - k + 4) % 4], ("g", color, k))
        i = 0 if k == 1 else 1
        block = g.at[color, (p - k + 4) % 4, pl.ds(64 * i, 64)]
        send(block, block, ("g2", color, k), dev(color, dp=k))

    def first_last(color):
        p, d = lines[color]
        for i, k in enumerate((1, 3)):
            arrive(g.at[color, (p + 2) % 4, pl.ds(64 * i, 64)], ("g2", color, k))

    slot_ids = lax.broadcasted_iota(jnp.int32, (SLOTS, 128), 0).astype(jnp.float32)

    def spread(color, k, weighted):
        p, d = lines[color]
        table = ibuf[color, (p + k) % 4]
        blocks = []
        for i in range(8):
            hit = table[i : i + 1] == slot_ids
            blocks.append(jnp.where(hit, table[8 + i : 9 + i] if weighted else 1.0, 0.0))
        return jnp.concatenate(blocks, axis=0)

    def dispatch(color, k):
        p, d = lines[color]
        seq = (p + k) % 4
        rows = jnp.dot(
            spread(color, k, False).astype(jnp.bfloat16), g[color, seq], preferred_element_type=jnp.float32
        ).astype(jnp.bfloat16)
        disp[color, k] = rows.reshape(4, 2, SLOTS, HALF)
        target = r.at[color, d, seq, core]
        for dd in (2, 1, -1):
            for to in range(2):
                src = disp.at[color, k, (d + dd + 4) % 4, to]
                send(src, target, ("d", color, k, dd), dev(color, dd=dd, to=to), width=2)
        send(disp.at[color, k, d, 1 - core], target, ("d", color, k, 0), sibling)
        local(disp.at[color, k, d, core], target, ("d", color, k, "here"))

    def arrivals(kind, color, k, dd, block):
        if dd == 0:
            arrive(block(core), (kind, color, k, "here"))
            arrive(block(1 - core), (kind, color, k, 0))
            return
        for from_core in range(2):
            arrive(block(from_core), (kind, color, k, 2 if dd == 2 else -dd), from_core)

    def group(index, xs, ys):
        places = [(kx, ky) for kx in xs for ky in ys]
        for kx, ky in places:
            column, row = (x + kx) % 4, (y + ky) % 4
            arrivals("d", 0, ky, STEP[kx], lambda c: r.at[0, column, row, c])
            arrivals("d", 1, kx, STEP[ky], lambda c: r.at[1, row, column, c])
        low = [r[0, (x + kx) % 4, (y + ky) % 4].reshape(2 * SLOTS, HALF) for kx, ky in places]
        high = [r[1, (y + ky) % 4, (x + kx) % 4].reshape(2 * SLOTS, HALF) for kx, ky in places]
        low, high = jnp.concatenate(low, axis=0), jnp.concatenate(high, axis=0)

        def product(weight):
            by_row = (((1,), (1,)), ((), ()))
            return lax.dot_general(
                low, weight[:, 0:HALF], by_row, preferred_element_type=jnp.float32
            ) + lax.dot_general(high, weight[:, HALF : 2 * HALF], by_row, preferred_element_type=jnp.float32)

        gate, up = product(wg), product(wu)
        inner = (gate / (1.0 + jnp.exp(-gate)) * up).astype(jnp.bfloat16)
        result = jnp.dot(inner, wd[...], preferred_element_type=jnp.float32).astype(jnp.bfloat16)
        res[0, index] = result[:, 0:HALF].reshape(4, 2, SLOTS, HALF)
        res[1, index] = result[:, HALF : 2 * HALF].reshape(4, 2, SLOTS, HALF)
        for i, (kx, ky) in enumerate(places):
            for color, kk, dd in ((0, ky, STEP[kx]), (1, kx, STEP[ky])):
                p, d = lines[color]
                target = cbuf.at[color, d, core, (p + kk) % 4]
                if dd == 0:
                    send(res.at[color, index, i, 1 - core], target, ("r", color, kk, 0), sibling)
                    local(res.at[color, index, i, core], target, ("r", color, kk, "here"))
                else:
                    for to in range(2):
                        src = res.at[color, index, i, to]
                        send(src, target, ("r", color, kk, dd), dev(color, dd=dd, to=to), width=2)

    def scales(color, k):
        scale = spread(color, k, True)
        high = scale.astype(jnp.bfloat16)
        return high, (scale - high.astype(jnp.float32)).astype(jnp.bfloat16)

    def combine(color, k, terms):
        p, d = lines[color]
        seq = (p + k) % 4
        for dd in (0, 1, -1, 2):
            arrivals("r", color, k, dd, lambda c: cbuf.at[color, (d + dd + 4) % 4, c, seq])
        rows = cbuf[color, :, :, pl.ds(seq, 1)].reshape(256, HALF)
        total = 0.0
        for term in terms:
            total = total + lax.dot_general(
                term, rows, (((0,), (0,)), ((), ())), preferred_element_type=jnp.float32
            )
        if k == 0:
            own_sum[color] = total
            return
        sbuf[color, k] = total.astype(jnp.bfloat16)
        send(sbuf.at[color, k], f.at[color, k], ("f", color, k), dev(color, dp=k))

    both = (0, 1)
    for color in both:
        dispatch(color, 0)
    for color in both:
        for k in (1, 3, 2):
            arrive(ibuf.at[color, (lines[color][0] - k + 4) % 4], ("info", color, k))
    for k in (1, 3):
        for color in both:
            first_near(color, k)
    for k in (1, 3):
        for color in both:
            dispatch(color, (4 - k) % 4)
    for color in both:
        first_last(color)
        dispatch(color, 2)
    before_groups = len(sent)
    arrive(wg, "wg")
    arrive(wu, "wu")
    arrive(wd, "wd")
    group(0, (1, 3), (1, 3))
    group(1, (0, 2), (1, 3))
    group(2, (1, 3), (0, 2))
    group(3, (0, 2), (0, 2))
    drain(before_groups)
    for color in both:
        for k in (1, 3):
            combine(color, k, scales(color, k))
    ready = {(color, k): scales(color, k) for k in (2, 0) for color in both}
    for k in (2, 0):
        for color in both:
            combine(color, k, ready[color, k])
    for color in (1, 0):
        cols = pl.ds(HALF * color, HALF)
        total = hidden[:, cols] + own_sum[color]
        for k in (1, 3, 2):
            arrive(f.at[color, k], ("f", color, k))
            total = total + f[color, k].astype(jnp.float32)
        out_ref[:, cols] = total.astype(out_ref.dtype)
    drain(len(sent))


def per_device(
    tokens,
    attention_gain,
    attention_in,
    attention_out,
    expert_gain,
    routes,
    route_weights,
    gate_weight,
    up_weight,
    down_weight,
):
    rows, model = tokens.shape
    width = gate_weight.shape[2]
    vmem = pl.BlockSpec(memory_space=pltpu.VMEM)
    hbm = pl.BlockSpec(memory_space=pl.ANY)
    blocks = (SLOTS, HALF)
    scratch = [
        (tokens.shape, jnp.bfloat16),
        ((1, model), jnp.float32),
        (attention_in.shape, jnp.bfloat16),
        (attention_out.shape, jnp.bfloat16),
        ((1, model), jnp.float32),
        (routes.shape[::-1], jnp.int32),
        (routes.shape[::-1], jnp.float32),
        ((8, 2, QKV), jnp.bfloat16),
        ((8, 2, HEAD_DIM), jnp.bfloat16),
        ((8, 2, QKV), jnp.bfloat16),
        ((8, 2, HEAD_DIM), jnp.bfloat16),
        ((NX, NZ, NY, 16, QKV), jnp.bfloat16),
        ((NX, NZ, NY, 16, HEAD_DIM), jnp.bfloat16),
        ((2, rows, model), jnp.bfloat16),
        ((rows, model), jnp.bfloat16),
        ((rows, model), jnp.bfloat16),
        ((rows, model), jnp.float32),
        ((width, model), jnp.bfloat16),
        ((width, model), jnp.bfloat16),
        ((width, model), jnp.bfloat16),
        ((2, 4, 16, rows), jnp.float32),
        ((2, 4, 16, rows), jnp.float32),
        ((2, 4, rows, HALF), jnp.bfloat16),
        ((2, 4, 4, 2) + blocks, jnp.bfloat16),
        ((2, 4, 4, 2) + blocks, jnp.bfloat16),
        ((2, 4, 4, 2) + blocks, jnp.bfloat16),
        ((2, 4, 2, 4) + blocks, jnp.bfloat16),
        ((2, 4, rows, HALF), jnp.bfloat16),
        ((2, 4, rows, HALF), jnp.bfloat16),
        ((2, rows, HALF), jnp.float32),
    ]
    mixed = pl.pallas_call(
        layer_kernel,
        out_shape=jax.ShapeDtypeStruct((rows, model), jnp.bfloat16),
        in_specs=[hbm] * 10,
        out_specs=vmem,
        scratch_shapes=[pltpu.VMEM(shape, dtype) for shape, dtype in scratch]
        + [pltpu.SemaphoreType.DMA((SENDS,)), pltpu.SemaphoreType.DMA((RECVS,))],
        compiler_params=pltpu.CompilerParams(collective_id=0, has_side_effects=True),
        name="layer",
    )(
        tokens,
        attention_gain.reshape(1, model),
        attention_in,
        attention_out,
        expert_gain.reshape(1, model),
        routes.T,
        route_weights.T,
        gate_weight[0].T,
        up_weight[0].T,
        down_weight[0],
    )
    return mixed.astype(jnp.bfloat16)


def solution(mesh):
    placed = (
        P(("fsdp", "expert"), None),
        P(),
        P(("fsdp", "expert"), None),
        P(("fsdp", "expert"), None),
        P(),
        P(("fsdp", "expert"), None),
        P(("fsdp", "expert"), None),
        P("expert", None, None),
        P("expert", None, None),
        P("expert", None, None),
    )
    return jax.shard_map(
        per_device,
        mesh=mesh,
        in_specs=placed,
        out_specs=P(("fsdp", "expert"), None),
        check_vma=False,
    )
```
